128 devices in a mesh: grp: 8 (over y, core), tm: 16 (over x, z).
Axes of the slice: x: 4, y: 4, z: 4, core: 2. Of those that a mesh axis runs over, the one named last changes fastest.
Arguments:
- raw: float32 [8192, 4096], P('grp', 'tm')
- channel_order: int32 [8, 1024], P('grp'), may hold values from 0 to 1023, each once within a row
- tile_list: int32 [255, 2], replicated, may hold values from 0 to 127, as said below
- tile_owner: int32 [255], replicated, may hold values from 0 to 127, as said below
Outputs:
- correlations: bfloat16 [256, 64, 64, 128], P(('grp', 'tm'))
The draws below stay inside these ranges and needn't reach their ends.
Inputs may be any that keep to these rules, and one draw needn't show every extreme that they name: Each row of channel_order is a permutation of 0 .. 1023. `tile_list`: the rows are the tiles (b, b) for every block b and (b, b + 1) for every b < 127, each once, in a drawn order. `tile_owner`: the owner of a tile (b, b + 1) is b; the owner of a tile (b, b) is b + 1 for b < 127, and the last block's diagonal tile is owned by 128 - 1; no owner holds more than 2 tiles, and owner 128 - 1 holds exactly 2.
All inputs are finite; a program needn't handle non-finite values.
Results may differ from the reference program's by a relative error of at most 0.013.
Values may be sent and summed in bfloat16 or wider, within the bound.
No kernel may reach another device: no remote copies, remote signals or barrier semaphores. Data moves between devices by JAX's collectives and lax.ppermute only.
A program may use at most 64 MiB of HBM per device.

```python
import math
import jax
import jax.numpy as jnp
from jax import lax

BLOCK_CH = 64
SEG_LEN = 256
BAND = 64
BAND_LO = 3
LAGS = 128
NORM_HALF = 64
TILE_CAP = 2
GROUPS = 8
GROUP_CH = 1024
CHANNELS = 8192
SEGS = 16
SAMPLES = 4096
BLOCKS = 128
TILES = 255


def draw_raw(key, part):
    key_noise = jax.random.fold_in(key, 0)
    key_gain = jax.random.fold_in(key, 1)
    key_level = jax.random.fold_in(key, 4)
    key_active = jax.random.fold_in(key, 5)
    gain = jnp.exp(jax.random.uniform(key_gain, (CHANNELS, 1), jnp.float32, 0.0, math.log(10.0)))
    level = jnp.exp(jax.random.uniform(key_level, (1, SAMPLES), jnp.float32, 0.0, math.log(3.0)))
    active_share = min(1.0, 6.0 / (2 * NORM_HALF + 1))
    active = jax.random.bernoulli(key_active, active_share, (CHANNELS, SAMPLES)).astype(jnp.float32)
    noise = jax.random.normal(key_noise, (CHANNELS, SAMPLES), jnp.float32)
    return noise * gain * level * active


def tile_pairs(key):
    block_index = jnp.arange(BLOCKS, dtype=jnp.int32)
    off_index = jnp.arange(BLOCKS - 1, dtype=jnp.int32)
    diag_owner = jnp.minimum(block_index + 1, BLOCKS - 1)
    off_owner = off_index
    first = jnp.concatenate([block_index, off_index])
    second = jnp.concatenate([block_index, off_index + 1])
    owner = jnp.concatenate([diag_owner, off_owner])
    order = jax.random.permutation(key, TILES)
    pairs = jnp.stack([first, second], axis=1)[order]
    return (pairs.astype(jnp.int32), owner[order].astype(jnp.int32))


def draw_tile_list(key, part):
    return tile_pairs(jax.random.fold_in(key, 7))[0]


def draw_tile_owner(key, part):
    return tile_pairs(jax.random.fold_in(key, 7))[1]


def setup_inputs(seed: int = 0) -> dict:
    keys = jax.random.split(jax.random.key(seed), 5)
    return {
        "raw": draw_raw(jax.random.fold_in(keys[4], 71), 0),
        "channel_order": jax.vmap(lambda own: jax.random.permutation(own, GROUP_CH))(jax.random.split(keys[1], GROUPS)).reshape((GROUPS, GROUP_CH)).astype(jnp.int32),
        "tile_list": draw_tile_list(jax.random.fold_in(keys[4], 71), 0),
        "tile_owner": draw_tile_owner(jax.random.fold_in(keys[4], 71), 0),
    }


def tables():
    sample = jnp.arange(SEG_LEN, dtype=jnp.int32)
    freq = BAND_LO + jnp.arange(BAND, dtype=jnp.int32)
    phase = sample[:, None] * freq[None, :] % SEG_LEN
    angle = phase.astype(jnp.float32) * (2.0 * math.pi / SEG_LEN)
    dft = jnp.concatenate([jnp.cos(angle), -jnp.sin(angle)], axis=1)
    offset = jnp.arange(BAND, dtype=jnp.int32)
    distance = jnp.abs(offset[:, None] - offset[None, :])
    weights = (BAND - distance).astype(jnp.float32)
    smooth = weights / lax.optimization_barrier(jnp.sum(weights, axis=0, keepdims=True))
    taper = 0.5 - 0.5 * jnp.cos((offset.astype(jnp.float32) + 0.5) * (2.0 * math.pi / BAND))
    lagged = jnp.arange(LAGS, dtype=jnp.int32) - LAGS // 2
    lag_phase = freq[:, None] * lagged[None, :] % SEG_LEN
    lag_angle = lag_phase.astype(jnp.float32) * (2.0 * math.pi / SEG_LEN)
    lag_table = jnp.concatenate([jnp.cos(lag_angle), -jnp.sin(lag_angle)], axis=0).astype(jnp.bfloat16)
    return (dft, smooth, taper, lag_table)

def window_mean(magnitude):
    width = 2 * NORM_HALF + 1
    padded = jnp.pad(magnitude, ((0, 0), (NORM_HALF + 1, NORM_HALF)))
    running = jnp.cumsum(padded, axis=1)
    return (running[:, width:] - running[:, :-width]) / width

def whiten(normed, dft, smooth, taper):
    rows, length = normed.shape
    pieces = normed.reshape(rows * (length // SEG_LEN), SEG_LEN)
    spectrum = jnp.dot(pieces, dft, precision=lax.Precision.HIGHEST, preferred_element_type=jnp.float32)
    real_part = spectrum[:, :BAND]
    imag_part = spectrum[:, BAND:]
    power = real_part * real_part + imag_part * imag_part
    smoothed = jnp.dot(power, smooth, precision=lax.Precision.HIGHEST, preferred_element_type=jnp.float32)
    factor = taper / jnp.sqrt(smoothed + 1e-06)
    white = spectrum * jnp.concatenate([factor, factor], axis=1)
    return white.astype(jnp.bfloat16).reshape(rows, length // SEG_LEN, 2 * BAND)

def reference(raw, channel_order, tile_list, tile_owner):
    dft, smooth, taper, lag_table = tables()
    rows = (jnp.arange(GROUPS, dtype=jnp.int32)[:, None] * GROUP_CH + channel_order).reshape(-1)
    ordered = jnp.take(raw, rows, axis=0)
    normed = ordered / (window_mean(jnp.abs(ordered)) + 1e-05)
    spectra = whiten(normed, dft, smooth, taper).reshape(BLOCKS, BLOCK_CH, SEGS, 2 * BAND)
    positions = jnp.arange(TILES, dtype=jnp.int32)
    same_owner = tile_owner[:, None] == tile_owner[None, :]
    slot_rank = lax.optimization_barrier(jnp.sum((same_owner & (positions[None, :] < positions[:, None])).astype(jnp.int32), axis=1))
    slot_of = tile_owner * TILE_CAP + slot_rank
    norm_scale = 1.0 / math.sqrt(SEGS * BAND)

    def one_slot(slot):
        match = slot_of == slot
        present = jnp.any(match)
        tile_id = jnp.sum(jnp.where(match, positions, 0))
        left = spectra[tile_list[tile_id, 0]].astype(jnp.float32)
        right = spectra[tile_list[tile_id, 1]].astype(jnp.float32)
        left_re = left[:, :, :BAND]
        left_im = left[:, :, BAND:]
        right_re = right[:, :, :BAND]
        right_im = right[:, :, BAND:]
        cross_re = jnp.einsum('asf,bsf->abf', left_re, right_re) + jnp.einsum('asf,bsf->abf', left_im, right_im)
        cross_im = jnp.einsum('asf,bsf->abf', left_im, right_re) - jnp.einsum('asf,bsf->abf', left_re, right_im)
        cross = jnp.concatenate([cross_re, cross_im], axis=2).astype(jnp.bfloat16)
        values = jnp.dot(cross.reshape(BLOCK_CH * BLOCK_CH, 2 * BAND), lag_table, preferred_element_type=jnp.float32) * norm_scale
        values = jnp.where(present, values, jnp.zeros_like(values))
        return values.astype(jnp.bfloat16).reshape(BLOCK_CH, BLOCK_CH, LAGS)
    return lax.map(one_slot, jnp.arange(BLOCKS * TILE_CAP, dtype=jnp.int32))
```

```python
import math

import jax
import jax.numpy as jnp
import numpy as np
from jax import lax
from jax.experimental import pallas as pl
from jax.experimental.pallas import tpu as pltpu
from jax.sharding import PartitionSpec as P

SEG_LEN = 256
BAND = 64
BAND_LO = 3
LAGS = 128
NORM_HALF = 64
TILE_CAP = 2
BLOCK = 64
SEGS = 16
HALF = BAND // 2
ROWS = SEGS * BLOCK
F32 = jnp.float32
BF16 = jnp.bfloat16


def split_bf16(values):
    high = values.astype(jnp.bfloat16)
    low = (values.astype(np.float32) - high.astype(np.float32)).astype(jnp.bfloat16)
    return high, low


def band_table():
    source = np.arange(2 * SEG_LEN) - SEG_LEN // 2
    target = np.arange(SEG_LEN)
    return (np.abs(source[:, None] - target[None, :]) <= NORM_HALF).astype(jnp.bfloat16)


def frequency_rows():
    row = np.arange(2 * BAND)
    upper, part, place = row // BAND, (row // HALF) % 2, row % HALF
    return upper * HALF + place, part


def dft_table():
    freq, part = frequency_rows()
    sample = np.arange(SEG_LEN)
    angle = ((freq[:, None] + BAND_LO) * sample[None, :] % SEG_LEN) * (2.0 * math.pi / SEG_LEN)
    table = np.where(part[:, None] == 0, np.cos(angle), -np.sin(angle)).astype(np.float32)
    return np.concatenate(split_bf16(table), axis=0)


def smooth_tables():
    freq, _ = frequency_rows()
    weights = (BAND - np.abs(freq[:, None] - freq[None, :])).astype(np.float32)
    band = np.arange(BAND)
    total = (BAND - np.abs(band[:, None] - band[None, :])).sum(axis=0).astype(np.float32)
    taper = 0.5 - 0.5 * np.cos((freq + 0.5) * (2.0 * math.pi / BAND))
    shape = (2 * BAND, 2 * BLOCK)
    scale = np.stack(
        [
            np.broadcast_to((1.0 / total[freq])[:, None], shape),
            np.broadcast_to(taper[:, None], shape),
        ]
    ).astype(np.float32)
    return np.concatenate([weights, weights], axis=1).astype(jnp.bfloat16), scale


def lag_table():
    row = np.arange(2 * BAND)
    upper, place, part = row // BAND, (row // 2) % HALF, row % 2
    freq = upper * HALF + place + BAND_LO
    lag = np.arange(LAGS) - LAGS // 2
    angle = (freq[:, None] * lag[None, :] % SEG_LEN) * (2.0 * math.pi / SEG_LEN)
    table = np.where(part[:, None] == 0, np.cos(angle), -np.sin(angle))
    table = table.astype(np.float32).astype(jnp.bfloat16).astype(np.float32)
    return (table / math.sqrt(SEGS * BAND)).astype(jnp.bfloat16)


def dot(left, right, left_dim=1, right_dim=0):
    return lax.dot_general(
        left, right, (((left_dim,), (right_dim,)), ((), ())), preferred_element_type=F32
    )


def low_lanes(shape):
    return lax.broadcasted_iota(jnp.int32, shape, 1) < BLOCK


def sort_kernel(order_ref, raw_ref, out_ref, raw_low):
    channels = raw_ref.shape[0]
    raw_low[...] = raw_ref[...].astype(BF16)
    lanes = lax.broadcasted_iota(jnp.int32, (128, 128), 1)
    for chunk in range(channels // 128):
        wanted = jnp.broadcast_to(order_ref[chunk : chunk + 1, :], (128, 128)).T
        pieces = [
            jnp.where(wanted == lanes + 128 * piece, 1.0, 0.0).astype(BF16)
            for piece in range(channels // 128)
        ]
        picked = dot(jnp.concatenate(pieces, axis=1), raw_low[...])
        out_ref[pl.ds(chunk * 128, 128), :] = picked.astype(BF16)


def sort_rows(raw, order):
    channels, samples = raw.shape
    return pl.pallas_call(
        sort_kernel,
        out_shape=jax.ShapeDtypeStruct((channels, samples), BF16),
        in_specs=[pl.BlockSpec(memory_space=pltpu.VMEM)] * 2,
        out_specs=pl.BlockSpec(memory_space=pltpu.VMEM),
        scratch_shapes=[pltpu.VMEM((channels, samples), BF16)],
        name="sort_rows",
    )(order.reshape(channels // 128, 128), raw)


def whiten_kernel(x_ref, band_ref, dft_ref, smooth_ref, scale_ref, out_ref, held):
    low = low_lanes((BAND, 2 * BLOCK))
    half_seg = SEG_LEN // 2
    for pair in range(SEGS // 2):
        start = pair * 2 * BLOCK
        x = x_ref[start : start + 2 * BLOCK, :].astype(F32)
        size = jnp.abs(x)
        blank = jnp.zeros((BLOCK, half_seg), F32)
        before = (
            jnp.abs(x_ref[start - BLOCK : start, half_seg:].astype(F32)) if pair > 0 else blank
        )
        stop = start + 2 * BLOCK
        after = (
            jnp.abs(x_ref[stop : stop + BLOCK, :half_seg].astype(F32))
            if pair < SEGS // 2 - 1
            else blank
        )
        before = jnp.concatenate([before, size[:BLOCK, half_seg:]], axis=0)
        after = jnp.concatenate([size[BLOCK:, :half_seg], after], axis=0)
        around = jnp.concatenate([before, size, after], axis=1).astype(BF16)
        mean = dot(around, band_ref[...]) * (1.0 / (2 * NORM_HALF + 1))
        normed = x / (mean + 1e-05)
        normed_high = normed.astype(BF16)
        normed_low = (normed - normed_high.astype(F32)).astype(BF16)
        both = dot(dft_ref[...], normed_high, 1, 1)
        spectrum = (both[: 2 * BAND] + both[2 * BAND :]) + dot(
            dft_ref[: 2 * BAND, :], normed_low, 1, 1
        )
        power = spectrum * spectrum
        power_high = power.astype(BF16)
        power_low = (power - power_high.astype(F32)).astype(BF16)
        smoothed = dot(smooth_ref[...], jnp.concatenate([power_high, power_low], axis=0))
        white = spectrum * (scale_ref[1] / jnp.sqrt(smoothed * scale_ref[0] + 1e-06))
        lower, upper = white[:BAND], white[BAND:]
        turned = pltpu.roll(jnp.where(low, upper, lower), BLOCK, 1)
        first = jnp.where(low, lower, turned)
        second = jnp.where(low, turned, upper)
        for segment, value in ((2 * pair, first), (2 * pair + 1, second)):
            for part in range(2):
                held[pl.ds(part * SEGS + segment, HALF, stride=2 * SEGS), :] = value[
                    part * HALF : (part + 1) * HALF
                ]
    out_ref[...] = held[...].astype(BF16)


def whiten(x):
    band, dft = band_table(), dft_table()
    smooth, scale = smooth_tables()
    return pl.pallas_call(
        whiten_kernel,
        out_shape=jax.ShapeDtypeStruct((ROWS, 2 * BLOCK), BF16),
        in_specs=[pl.BlockSpec(memory_space=pltpu.VMEM)] * 5,
        out_specs=pl.BlockSpec(memory_space=pltpu.VMEM),
        scratch_shapes=[pltpu.VMEM((ROWS, 2 * BLOCK), F32)],
        name="whiten",
    )(x, band, dft, smooth, scale)


def fill_cross(left_ref, right_ref, cross, left_twice=False):
    low = low_lanes((2 * SEGS, 2 * BLOCK))
    for place in range(HALF):
        start = place * 2 * SEGS
        left = left_ref[start : start + 2 * SEGS, :].astype(F32)
        right = right_ref[start : start + 2 * SEGS, :].astype(F32)
        right = jnp.where(left_twice, left, right)
        other = jnp.concatenate([left[SEGS:], -left[:SEGS]], axis=0)
        turned = pltpu.roll(jnp.where(low, other, left), BLOCK, 1)
        rows = jnp.concatenate(
            [jnp.where(low, left, turned), jnp.where(low, turned, other)], axis=0
        ).astype(BF16)
        columns = jnp.concatenate(
            [jnp.where(low, right, 0.0), jnp.where(low, 0.0, right)], axis=0
        ).astype(BF16)
        cross[place * 2 * BLOCK : (place + 1) * 2 * BLOCK, :] = dot(rows, columns, 0, 0)


def tile_kernel(tiles_ref, own_ref, before_ref, after_ref, lag_ref, out_ref, cross, stage, sem):
    own = lax.axis_index("grp") * lax.axis_size("tm") + lax.axis_index("tm")
    last = lax.axis_size("grp") * lax.axis_size("tm") - 1
    tiles = tiles_ref[...]
    position = lax.broadcasted_iota(jnp.int32, (tiles.shape[0], 1), 0)

    def place_of(first, second):
        found = (tiles[:, 0:1] == first) & (tiles[:, 1:2] == second)
        return jnp.sum(jnp.where(found, position, 0))

    diagonal = place_of(own - 1, own - 1)
    other = place_of(own, jnp.minimum(own + 1, last))
    diagonal_first = (own > 0) & (diagonal < other)
    low = low_lanes((2 * HALF, 2 * BLOCK))

    def lags(number, slot):
        for pair in range(BLOCK // 2):
            first = cross[pl.ds(2 * pair, 2 * HALF, stride=BLOCK), :]
            second = cross[pl.ds(2 * pair + 1, 2 * HALF, stride=BLOCK), :]
            turned = pltpu.roll(jnp.where(low, second, first), BLOCK, 1)
            both = jnp.concatenate(
                [jnp.where(low, first, turned), jnp.where(low, turned, second)], axis=0
            ).astype(BF16)
            stage[number, 2 * pair * BLOCK : 2 * (pair + 1) * BLOCK, :] = dot(
                both, lag_ref[...], 0, 0
            ).astype(BF16)
        pltpu.make_async_copy(stage.at[number], out_ref.at[slot], sem.at[number]).start()

    first_slot = jnp.where(diagonal_first, 0, 1)
    fill_cross(before_ref, before_ref, cross)
    lags(0, first_slot)
    fill_cross(own_ref, after_ref, cross, own == last)
    lags(1, 1 - first_slot)
    pltpu.make_async_copy(stage.at[0], out_ref.at[first_slot], sem.at[0]).wait()
    pltpu.make_async_copy(stage.at[1], out_ref.at[1 - first_slot], sem.at[1]).wait()


def correlate(tiles, own, before, after):
    vmem = pl.BlockSpec(memory_space=pltpu.VMEM)
    return pl.pallas_call(
        tile_kernel,
        out_shape=jax.ShapeDtypeStruct((TILE_CAP, BLOCK * BLOCK, LAGS), BF16),
        in_specs=[vmem] * 5,
        out_specs=pl.BlockSpec(memory_space=pl.ANY),
        scratch_shapes=[
            pltpu.VMEM((HALF * 2 * BLOCK, 2 * BLOCK), F32),
            pltpu.VMEM((TILE_CAP, BLOCK * BLOCK, LAGS), BF16),
            pltpu.SemaphoreType.DMA((TILE_CAP,)),
        ],
        name="correlate",
    )(tiles, own, before, after, lag_table())


def per_device(raw, channel_order, tile_list, tile_owner):
    count = lax.axis_size("grp") * lax.axis_size("tm")
    ordered = sort_rows(raw, channel_order[0])
    parts = ordered.reshape(SEGS, BLOCK, SEG_LEN)
    record = lax.all_to_all(parts, "tm", split_axis=0, concat_axis=0, tiled=True)
    own = whiten(record.reshape(ROWS, SEG_LEN))
    up = [(i, i + 1) for i in range(count - 1)]
    down = [(i + 1, i) for i in range(count - 1)]
    before = lax.ppermute(own, ("grp", "tm"), up)
    after = lax.ppermute(own, ("grp", "tm"), down)
    out = correlate(tile_list, own, before, after)
    return out.reshape(TILE_CAP, BLOCK, BLOCK, LAGS)


def solution(mesh):
    return jax.shard_map(
        per_device,
        mesh=mesh,
        in_specs=(P("grp", "tm"), P("grp", None), P(), P()),
        out_specs=P(("grp", "tm"), None, None, None),
        check_vma=False,
    )
```

```python
import math

import jax
import jax.numpy as jnp
import numpy as np
from jax import lax
from jax.experimental import pallas as pl
from jax.experimental.pallas import tpu as pltpu
from jax.sharding import PartitionSpec as P

SEG_LEN = 256
BAND = 64
BAND_LO = 3
LAGS = 128
NORM_HALF = 64
TILE_CAP = 2
BLOCK = 64
SEGS = 16
HALF = BAND // 2
ROWS = SEGS * BLOCK
F32 = jnp.float32
BF16 = jnp.bfloat16


def split_bf16(values):
    high = values.astype(jnp.bfloat16)
    low = (values.astype(np.float32) - high.astype(np.float32)).astype(jnp.bfloat16)
    return high, low


def band_table():
    source = np.arange(2 * SEG_LEN) - SEG_LEN // 2
    target = np.arange(SEG_LEN)
    return (np.abs(source[:, None] - target[None, :]) <= NORM_HALF).astype(jnp.bfloat16)


def frequency_rows():
    row = np.arange(2 * BAND)
    upper, part, place = row // BAND, (row // HALF) % 2, row % HALF
    return upper * HALF + place, part


def dft_table():
    freq, part = frequency_rows()
    sample = np.arange(SEG_LEN)
    angle = ((freq[:, None] + BAND_LO) * sample[None, :] % SEG_LEN) * (2.0 * math.pi / SEG_LEN)
    table = np.where(part[:, None] == 0, np.cos(angle), -np.sin(angle)).astype(np.float32)
    return np.concatenate(split_bf16(table), axis=0)


def smooth_tables():
    freq, _ = frequency_rows()
    weights = (BAND - np.abs(freq[:, None] - freq[None, :])).astype(np.float32)
    band = np.arange(BAND)
    total = (BAND - np.abs(band[:, None] - band[None, :])).sum(axis=0).astype(np.float32)
    taper = 0.5 - 0.5 * np.cos((freq + 0.5) * (2.0 * math.pi / BAND))
    shape = (2 * BAND, 2 * BLOCK)
    scale = np.stack(
        [
            np.broadcast_to((1.0 / total[freq])[:, None], shape),
            np.broadcast_to(taper[:, None], shape),
        ]
    ).astype(np.float32)
    return np.concatenate([weights, weights], axis=1).astype(jnp.bfloat16), scale


def lag_table():
    row = np.arange(2 * BAND)
    upper, place, part = row // BAND, (row // 2) % HALF, row % 2
    freq = upper * HALF + place + BAND_LO
    lag = np.arange(LAGS) - LAGS // 2
    angle = (freq[:, None] * lag[None, :] % SEG_LEN) * (2.0 * math.pi / SEG_LEN)
    table = np.where(part[:, None] == 0, np.cos(angle), -np.sin(angle))
    table = table.astype(np.float32).astype(jnp.bfloat16).astype(np.float32)
    return (table / math.sqrt(SEGS * BAND)).astype(jnp.bfloat16)


def dot(left, right, left_dim=1, right_dim=0):
    return lax.dot_general(
        left, right, (((left_dim,), (right_dim,)), ((), ())), preferred_element_type=F32
    )


def low_lanes(shape):
    return lax.broadcasted_iota(jnp.int32, shape, 1) < BLOCK


def sort_kernel(order_ref, raw_ref, out_ref, raw_low):
    channels = raw_ref.shape[0]
    raw_low[...] = raw_ref[...].astype(BF16)
    lanes = lax.broadcasted_iota(jnp.int32, (128, 128), 1)
    for chunk in range(channels // 128):
        wanted = jnp.broadcast_to(order_ref[chunk : chunk + 1, :], (128, 128)).T
        pieces = [
            jnp.where(wanted == lanes + 128 * piece, 1.0, 0.0).astype(BF16)
            for piece in range(channels // 128)
        ]
        picked = dot(jnp.concatenate(pieces, axis=1), raw_low[...])
        out_ref[pl.ds(chunk * 128, 128), :] = picked.astype(BF16)


def sort_rows(raw, order):
    channels, samples = raw.shape
    return pl.pallas_call(
        sort_kernel,
        out_shape=jax.ShapeDtypeStruct((channels, samples), BF16),
        in_specs=[pl.BlockSpec(memory_space=pltpu.VMEM)] * 2,
        out_specs=pl.BlockSpec(memory_space=pltpu.VMEM),
        scratch_shapes=[pltpu.VMEM((channels, samples), BF16)],
        name="sort_rows",
    )(order.reshape(channels // 128, 128), raw)


def whiten_kernel(x_ref, band_ref, dft_ref, smooth_ref, scale_ref, out_ref, held):
    low = low_lanes((BAND, 2 * BLOCK))
    half_seg = SEG_LEN // 2
    for pair in range(SEGS // 2):
        start = pair * 2 * BLOCK
        x = x_ref[start : start + 2 * BLOCK, :].astype(F32)
        size = jnp.abs(x)
        blank = jnp.zeros((BLOCK, half_seg), F32)
        before = (
            jnp.abs(x_ref[start - BLOCK : start, half_seg:].astype(F32)) if pair > 0 else blank
        )
        stop = start + 2 * BLOCK
        after = (
            jnp.abs(x_ref[stop : stop + BLOCK, :half_seg].astype(F32))
            if pair < SEGS // 2 - 1
            else blank
        )
        before = jnp.concatenate([before, size[:BLOCK, half_seg:]], axis=0)
        after = jnp.concatenate([size[BLOCK:, :half_seg], after], axis=0)
        around = jnp.concatenate([before, size, after], axis=1).astype(BF16)
        mean = dot(around, band_ref[...]) * (1.0 / (2 * NORM_HALF + 1))
        normed = x / (mean + 1e-05)
        normed_high = normed.astype(BF16)
        normed_low = (normed - normed_high.astype(F32)).astype(BF16)
        both = dot(dft_ref[...], normed_high, 1, 1)
        spectrum = (both[: 2 * BAND] + both[2 * BAND :]) + dot(
            dft_ref[: 2 * BAND, :], normed_low, 1, 1
        )
        power = spectrum * spectrum
        power_high = power.astype(BF16)
        power_low = (power - power_high.astype(F32)).astype(BF16)
        smoothed = dot(smooth_ref[...], jnp.concatenate([power_high, power_low], axis=0))
        white = spectrum * (scale_ref[1] / jnp.sqrt(smoothed * scale_ref[0] + 1e-06))
        lower, upper = white[:BAND], white[BAND:]
        turned = pltpu.roll(jnp.where(low, upper, lower), BLOCK, 1)
        first = jnp.where(low, lower, turned)
        second = jnp.where(low, turned, upper)
        for segment, value in ((2 * pair, first), (2 * pair + 1, second)):
            for part in range(2):
                held[pl.ds(part * SEGS + segment, HALF, stride=2 * SEGS), :] = value[
                    part * HALF : (part + 1) * HALF
                ]
    out_ref[...] = held[...].astype(BF16)


def whiten(x):
    band, dft = band_table(), dft_table()
    smooth, scale = smooth_tables()
    return pl.pallas_call(
        whiten_kernel,
        out_shape=jax.ShapeDtypeStruct((ROWS, 2 * BLOCK), BF16),
        in_specs=[pl.BlockSpec(memory_space=pltpu.VMEM)] * 5,
        out_specs=pl.BlockSpec(memory_space=pltpu.VMEM),
        scratch_shapes=[pltpu.VMEM((ROWS, 2 * BLOCK), F32)],
        name="whiten",
    )(x, band, dft, smooth, scale)


def fill_cross(left_at, right_at, cross):
    low = low_lanes((2 * SEGS, 2 * BLOCK))
    for place in range(HALF):
        rows = pl.ds(place * 2 * SEGS, 2 * SEGS)
        left = left_at(rows).astype(F32)
        right = right_at(rows).astype(F32)
        other = jnp.concatenate([left[SEGS:], -left[:SEGS]], axis=0)
        turned = pltpu.roll(jnp.where(low, other, left), BLOCK, 1)
        left = jnp.concatenate(
            [jnp.where(low, left, turned), jnp.where(low, turned, other)], axis=0
        ).astype(BF16)
        right = jnp.concatenate(
            [jnp.where(low, right, 0.0), jnp.where(low, 0.0, right)], axis=0
        ).astype(BF16)
        cross[place * 2 * BLOCK : (place + 1) * 2 * BLOCK, :] = dot(left, right, 0, 0)


def fill_lags(cross, lag_ref, stage):
    low = low_lanes((2 * HALF, 2 * BLOCK))
    for pair in range(BLOCK // 2):
        first = cross[pl.ds(2 * pair, 2 * HALF, stride=BLOCK), :]
        second = cross[pl.ds(2 * pair + 1, 2 * HALF, stride=BLOCK), :]
        turned = pltpu.roll(jnp.where(low, second, first), BLOCK, 1)
        both = jnp.concatenate(
            [jnp.where(low, first, turned), jnp.where(low, turned, second)], axis=0
        ).astype(BF16)
        rows = slice(2 * pair * BLOCK, 2 * (pair + 1) * BLOCK)
        stage[rows, :] = dot(both, lag_ref[...], 0, 0).astype(BF16)


def diagonal_slot(tiles_ref, own, last):
    position = lax.broadcasted_iota(jnp.int32, (1, tiles_ref.shape[1]), 1)

    def place_of(first, second):
        found = (tiles_ref[0:1, :] == first) & (tiles_ref[1:2, :] == second)
        return jnp.sum(jnp.where(found, position, 0))

    diagonal = place_of(own - 1, own - 1)
    other = place_of(own, jnp.minimum(own + 1, last))
    return jnp.where((own > 0) & (diagonal < other), 0, 1)


def tile_kernel(swap, tiles_ref, own_ref, other_ref, lag_ref, *rest):
    out_ref, cross, stage, sem = rest[-4:]
    own = lax.axis_index("grp") * lax.axis_size("tm") + lax.axis_index("tm")
    last = lax.axis_size("grp") * lax.axis_size("tm") - 1
    is_diagonal = own % 2 == (1 if swap == 0 else 0)
    no_other = (own == last) if swap == 1 else False

    def left_at(rows):
        return jnp.where(is_diagonal, other_ref[rows, :].astype(F32), own_ref[rows, :].astype(F32))

    def right_at(rows):
        if swap == 0:
            return other_ref[rows, :]
        return jnp.where(no_other, own_ref[rows, :].astype(F32), other_ref[rows, :].astype(F32))

    fill_cross(left_at, right_at, cross)
    fill_lags(cross, lag_ref, stage)
    slot = diagonal_slot(tiles_ref, own, last)
    slot = jnp.where(is_diagonal, slot, 1 - slot)
    copy = pltpu.make_async_copy(stage, out_ref.at[slot], sem)
    copy.start()
    copy.wait()


def correlate(swap, tiles, own, other, held=()):
    vmem = pl.BlockSpec(memory_space=pltpu.VMEM)
    anywhere = pl.BlockSpec(memory_space=pl.ANY)
    return pl.pallas_call(
        lambda *refs: tile_kernel(swap, *refs),
        out_shape=jax.ShapeDtypeStruct((TILE_CAP, BLOCK * BLOCK, LAGS), BF16),
        in_specs=[vmem] * 4 + [anywhere] * len(held),
        out_specs=anywhere,
        scratch_shapes=[
            pltpu.VMEM((HALF * 2 * BLOCK, 2 * BLOCK), F32),
            pltpu.VMEM((BLOCK * BLOCK, LAGS), BF16),
            pltpu.SemaphoreType.DMA,
        ],
        input_output_aliases={4: 0} if held else {},
        name=f"correlate_{swap}",
    )(tiles, own, other, lag_table(), *held)


def per_device(raw, channel_order, tile_list, tile_owner):
    count = lax.axis_size("grp") * lax.axis_size("tm")
    ordered = sort_rows(raw, channel_order[0])
    parts = ordered.reshape(SEGS, BLOCK, SEG_LEN)
    record = lax.all_to_all(parts, "tm", split_axis=0, concat_axis=0, tiled=True)
    own = whiten(record.reshape(ROWS, SEG_LEN))
    pairs = [(i, i ^ 1) for i in range(count)]
    shifted = [(i, i + 1 if i % 2 else i - 1) for i in range(1, count - 1)]
    near = lax.ppermute(own, ("grp", "tm"), pairs)
    far = lax.ppermute(own, ("grp", "tm"), shifted)
    tiles = tile_list.T
    out = correlate(0, tiles, own, near)
    out = correlate(1, tiles, own, far, (out,))
    return out.reshape(TILE_CAP, BLOCK, BLOCK, LAGS)


def solution(mesh):
    return jax.shard_map(
        per_device,
        mesh=mesh,
        in_specs=(P("grp", "tm"), P("grp", None), P(), P()),
        out_specs=P(("grp", "tm"), None, None, None),
        check_vma=False,
    )
```

```python
import math

import jax
import jax.numpy as jnp
import numpy as np
from jax import lax
from jax.experimental import pallas as pl
from jax.experimental.pallas import tpu as pltpu
from jax.sharding import PartitionSpec as P

SEG_LEN = 256
BAND = 64
BAND_LO = 3
LAGS = 128
NORM_HALF = 64
TILE_CAP = 2
BLOCK = 64
SEGS = 16
HALF = BAND // 2
ROWS = SEGS * BLOCK
F32 = jnp.float32
BF16 = jnp.bfloat16


def split_bf16(values):
    high = values.astype(jnp.bfloat16)
    low = (values.astype(np.float32) - high.astype(np.float32)).astype(jnp.bfloat16)
    return high, low


def band_table():
    source = np.arange(2 * SEG_LEN) - SEG_LEN // 2
    target = np.arange(SEG_LEN)
    return (np.abs(source[:, None] - target[None, :]) <= NORM_HALF).astype(jnp.bfloat16)


def frequency_rows():
    row = np.arange(2 * BAND)
    upper, part, place = row // BAND, (row // HALF) % 2, row % HALF
    return upper * HALF + place, part


def dft_table():
    freq, part = frequency_rows()
    sample = np.arange(SEG_LEN)
    angle = ((freq[:, None] + BAND_LO) * sample[None, :] % SEG_LEN) * (2.0 * math.pi / SEG_LEN)
    table = np.where(part[:, None] == 0, np.cos(angle), -np.sin(angle)).astype(np.float32)
    return np.concatenate(split_bf16(table), axis=0)


def smooth_tables():
    freq, _ = frequency_rows()
    weights = (BAND - np.abs(freq[:, None] - freq[None, :])).astype(np.float32)
    band = np.arange(BAND)
    total = (BAND - np.abs(band[:, None] - band[None, :])).sum(axis=0).astype(np.float32)
    taper = 0.5 - 0.5 * np.cos((freq + 0.5) * (2.0 * math.pi / BAND))
    shape = (2 * BAND, 2 * BLOCK)
    scale = np.stack(
        [
            np.broadcast_to((1.0 / total[freq])[:, None], shape),
            np.broadcast_to(taper[:, None], shape),
        ]
    ).astype(np.float32)
    return np.concatenate([weights, weights], axis=1).astype(jnp.bfloat16), scale


def lag_table():
    row = np.arange(2 * BAND)
    upper, place, part = row // BAND, (row // 2) % HALF, row % 2
    freq = upper * HALF + place + BAND_LO
    lag = np.arange(LAGS) - LAGS // 2
    angle = (freq[:, None] * lag[None, :] % SEG_LEN) * (2.0 * math.pi / SEG_LEN)
    table = np.where(part[:, None] == 0, np.cos(angle), -np.sin(angle))
    table = table.astype(np.float32).astype(jnp.bfloat16).astype(np.float32)
    return (table / math.sqrt(SEGS * BAND)).astype(jnp.bfloat16)


def in_vmem(array):
    return pltpu.with_memory_space_constraint(array, pltpu.VMEM)


def dot(left, right, left_dim=1, right_dim=0):
    return lax.dot_general(
        left, right, (((left_dim,), (right_dim,)), ((), ())), preferred_element_type=F32
    )


def low_lanes(shape):
    return lax.broadcasted_iota(jnp.int32, shape, 1) < BLOCK


def sort_kernel(order_ref, raw_ref, out_ref, raw_low):
    channels = raw_ref.shape[0]
    raw_low[...] = raw_ref[...].astype(BF16)
    lanes = lax.broadcasted_iota(jnp.int32, (128, 128), 1)
    for chunk in range(channels // 128):
        wanted = jnp.broadcast_to(order_ref[chunk : chunk + 1, :], (128, 128)).T
        pieces = [
            jnp.where(wanted == lanes + 128 * piece, 1.0, 0.0).astype(BF16)
            for piece in range(channels // 128)
        ]
        picked = dot(jnp.concatenate(pieces, axis=1), raw_low[...])
        out_ref[pl.ds(chunk * 128, 128), :] = picked.astype(BF16)


def sort_rows(raw, order):
    channels, samples = raw.shape
    return pl.pallas_call(
        sort_kernel,
        out_shape=pltpu.VMEM((channels, samples), BF16),
        in_specs=[pl.BlockSpec(memory_space=pltpu.VMEM)] * 2,
        out_specs=pl.BlockSpec(memory_space=pltpu.VMEM),
        scratch_shapes=[pltpu.VMEM((channels, samples), BF16)],
        name="sort_rows",
    )(order.reshape(channels // 128, 128), raw)


def whiten_kernel(x_ref, band_ref, dft_ref, smooth_ref, scale_ref, out_ref, held):
    low = low_lanes((BAND, 2 * BLOCK))
    half_seg = SEG_LEN // 2
    for pair in range(SEGS // 2):
        start = pair * 2 * BLOCK
        x = x_ref[start : start + 2 * BLOCK, :].astype(F32)
        size = jnp.abs(x)
        blank = jnp.zeros((BLOCK, half_seg), F32)
        before = (
            jnp.abs(x_ref[start - BLOCK : start, half_seg:].astype(F32)) if pair > 0 else blank
        )
        stop = start + 2 * BLOCK
        after = (
            jnp.abs(x_ref[stop : stop + BLOCK, :half_seg].astype(F32))
            if pair < SEGS // 2 - 1
            else blank
        )
        before = jnp.concatenate([before, size[:BLOCK, half_seg:]], axis=0)
        after = jnp.concatenate([size[BLOCK:, :half_seg], after], axis=0)
        around = jnp.concatenate([before, size, after], axis=1).astype(BF16)
        mean = dot(around, band_ref[...]) * (1.0 / (2 * NORM_HALF + 1))
        normed = x / (mean + 1e-05)
        normed_high = normed.astype(BF16)
        normed_low = (normed - normed_high.astype(F32)).astype(BF16)
        both = dot(dft_ref[...], normed_high, 1, 1)
        spectrum = (both[: 2 * BAND] + both[2 * BAND :]) + dot(
            dft_ref[: 2 * BAND, :], normed_low, 1, 1
        )
        power = spectrum * spectrum
        power_high = power.astype(BF16)
        power_low = (power - power_high.astype(F32)).astype(BF16)
        smoothed = dot(smooth_ref[...], jnp.concatenate([power_high, power_low], axis=0))
        white = spectrum * (scale_ref[1] / jnp.sqrt(smoothed * scale_ref[0] + 1e-06))
        lower, upper = white[:BAND], white[BAND:]
        turned = pltpu.roll(jnp.where(low, upper, lower), BLOCK, 1)
        first = jnp.where(low, lower, turned)
        second = jnp.where(low, turned, upper)
        for segment, value in ((2 * pair, first), (2 * pair + 1, second)):
            for part in range(2):
                held[pl.ds(part * SEGS + segment, HALF, stride=2 * SEGS), :] = value[
                    part * HALF : (part + 1) * HALF
                ]
    out_ref[...] = held[...].astype(BF16)


def whiten(x):
    band, dft = band_table(), dft_table()
    smooth, scale = smooth_tables()
    return pl.pallas_call(
        whiten_kernel,
        out_shape=pltpu.VMEM((ROWS, 2 * BLOCK), BF16),
        in_specs=[pl.BlockSpec(memory_space=pltpu.VMEM)] * 5,
        out_specs=pl.BlockSpec(memory_space=pltpu.VMEM),
        scratch_shapes=[pltpu.VMEM((ROWS, 2 * BLOCK), F32)],
        name="whiten",
    )(x, *(in_vmem(jnp.asarray(table)) for table in (band, dft, smooth, scale)))


def fill_cross(left_at, right_at, cross):
    low = low_lanes((2 * SEGS, 2 * BLOCK))
    for place in range(HALF):
        rows = pl.ds(place * 2 * SEGS, 2 * SEGS)
        left = left_at(rows).astype(F32)
        right = right_at(rows).astype(F32)
        other = jnp.concatenate([left[SEGS:], -left[:SEGS]], axis=0)
        turned = pltpu.roll(jnp.where(low, other, left), BLOCK, 1)
        left = jnp.concatenate(
            [jnp.where(low, left, turned), jnp.where(low, turned, other)], axis=0
        ).astype(BF16)
        right = jnp.concatenate(
            [jnp.where(low, right, 0.0), jnp.where(low, 0.0, right)], axis=0
        ).astype(BF16)
        cross[place * 2 * BLOCK : (place + 1) * 2 * BLOCK, :] = dot(left, right, 0, 0)


def fill_lags(cross, lag_ref, stage):
    low = low_lanes((2 * HALF, 2 * BLOCK))
    for pair in range(BLOCK // 2):
        first = cross[pl.ds(2 * pair, 2 * HALF, stride=BLOCK), :]
        second = cross[pl.ds(2 * pair + 1, 2 * HALF, stride=BLOCK), :]
        turned = pltpu.roll(jnp.where(low, second, first), BLOCK, 1)
        both = jnp.concatenate(
            [jnp.where(low, first, turned), jnp.where(low, turned, second)], axis=0
        ).astype(BF16)
        rows = slice(2 * pair * BLOCK, 2 * (pair + 1) * BLOCK)
        stage[rows, :] = dot(both, lag_ref[...], 0, 0).astype(BF16)


def diagonal_slot(tiles_ref, own, last):
    position = lax.broadcasted_iota(jnp.int32, (1, tiles_ref.shape[1]), 1)

    def place_of(first, second):
        found = (tiles_ref[0:1, :] == first) & (tiles_ref[1:2, :] == second)
        return jnp.sum(jnp.where(found, position, 0))

    diagonal = place_of(own - 1, own - 1)
    other = place_of(own, jnp.minimum(own + 1, last))
    return jnp.where((own > 0) & (diagonal < other), 0, 1)


def tile_kernel(swap, tiles_ref, own_ref, other_ref, lag_ref, *rest):
    out_ref, cross, stage, sem = rest[-4:]
    own = lax.axis_index("grp") * lax.axis_size("tm") + lax.axis_index("tm")
    last = lax.axis_size("grp") * lax.axis_size("tm") - 1
    is_diagonal = own % 2 == (1 if swap == 0 else 0)
    no_other = (own == last) if swap == 1 else False

    def left_at(rows):
        return jnp.where(is_diagonal, other_ref[rows, :].astype(F32), own_ref[rows, :].astype(F32))

    def right_at(rows):
        if swap == 0:
            return other_ref[rows, :]
        return jnp.where(no_other, own_ref[rows, :].astype(F32), other_ref[rows, :].astype(F32))

    fill_cross(left_at, right_at, cross)
    fill_lags(cross, lag_ref, stage)
    slot = diagonal_slot(tiles_ref, own, last)
    slot = jnp.where(is_diagonal, slot, 1 - slot)
    copy = pltpu.make_async_copy(stage, out_ref.at[slot], sem)
    copy.start()
    copy.wait()


def correlate(swap, tiles, own, other, held=()):
    vmem = pl.BlockSpec(memory_space=pltpu.VMEM)
    anywhere = pl.BlockSpec(memory_space=pl.ANY)
    return pl.pallas_call(
        lambda *refs: tile_kernel(swap, *refs),
        out_shape=jax.ShapeDtypeStruct((TILE_CAP, BLOCK * BLOCK, LAGS), BF16),
        in_specs=[vmem] * 4 + [anywhere] * len(held),
        out_specs=anywhere,
        scratch_shapes=[
            pltpu.VMEM((HALF * 2 * BLOCK, 2 * BLOCK), F32),
            pltpu.VMEM((BLOCK * BLOCK, LAGS), BF16),
            pltpu.SemaphoreType.DMA,
        ],
        input_output_aliases={4: 0} if held else {},
        name=f"correlate_{swap}",
    )(tiles, own, other, in_vmem(jnp.asarray(lag_table())), *held)


def per_device(raw, channel_order, tile_list, tile_owner):
    count = lax.axis_size("grp") * lax.axis_size("tm")
    ordered = sort_rows(raw, channel_order[0])
    parts = ordered.reshape(SEGS, BLOCK, SEG_LEN)
    record = lax.all_to_all(parts, "tm", split_axis=0, concat_axis=0, tiled=True)
    record = in_vmem(record.reshape(ROWS, SEG_LEN))
    own = in_vmem(whiten(record))
    pairs = [(i, i ^ 1) for i in range(count)]
    shifted = [(i, i + 1 if i % 2 else i - 1) for i in range(1, count - 1)]
    near = in_vmem(lax.ppermute(own, ("grp", "tm"), pairs))
    far = in_vmem(lax.ppermute(own, ("grp", "tm"), shifted))
    tiles = in_vmem(tile_list.T)
    out = correlate(0, tiles, own, near)
    out = correlate(1, tiles, own, far, (out,))
    return out.reshape(TILE_CAP, BLOCK, BLOCK, LAGS)


def solution(mesh):
    return jax.shard_map(
        per_device,
        mesh=mesh,
        in_specs=(P("grp", "tm"), P("grp", None), P(), P()),
        out_specs=P(("grp", "tm"), None, None, None),
        check_vma=False,
    )
```

```python
import math

import jax
import jax.numpy as jnp
import numpy as np
from jax import lax
from jax.experimental import pallas as pl
from jax.experimental.pallas import tpu as pltpu
from jax.sharding import PartitionSpec as P

SEG_LEN = 256
BAND = 64
BAND_LO = 3
LAGS = 128
NORM_HALF = 64
TILE_CAP = 2
BLOCK = 64
SEGS = 16
HALF = BAND // 2
PITCH = 72
STEP = 4
ROWS = SEGS * BLOCK
F32 = jnp.float32
BF16 = jnp.bfloat16


def split_bf16(values):
    high = values.astype(jnp.bfloat16)
    low = (values.astype(np.float32) - high.astype(np.float32)).astype(jnp.bfloat16)
    return high, low


def band_table():
    source = np.arange(2 * SEG_LEN) - SEG_LEN // 2
    target = np.arange(SEG_LEN)
    return (np.abs(source[:, None] - target[None, :]) <= NORM_HALF).astype(jnp.bfloat16)


def frequency_rows():
    row = np.arange(2 * BAND)
    upper, part, place = row // BAND, (row // HALF) % 2, row % HALF
    return upper * HALF + place, part


def dft_table():
    freq, part = frequency_rows()
    sample = np.arange(SEG_LEN)
    angle = (sample[:, None] * (freq[None, :] + BAND_LO) % SEG_LEN) * (2.0 * math.pi / SEG_LEN)
    table = np.where(part[None, :] == 0, np.cos(angle), -np.sin(angle)).astype(np.float32)
    return np.concatenate(split_bf16(table), axis=1)


def smooth_tables():
    freq, _ = frequency_rows()
    weights = (BAND - np.abs(freq[:, None] - freq[None, :])).astype(np.float32)
    band = np.arange(BAND)
    total = (BAND - np.abs(band[:, None] - band[None, :])).sum(axis=0).astype(np.float32)
    taper = 0.5 - 0.5 * np.cos((freq + 0.5) * (2.0 * math.pi / BAND))
    scale = np.stack([1.0 / total[freq], taper] * 4).astype(np.float32)
    return weights.astype(jnp.bfloat16), scale


def lag_table():
    row = np.arange(2 * BAND)
    upper, place, part = row // BAND, (row // 2) % HALF, row % 2
    freq = upper * HALF + place + BAND_LO
    lag = np.arange(LAGS) - LAGS // 2
    angle = (freq[:, None] * lag[None, :] % SEG_LEN) * (2.0 * math.pi / SEG_LEN)
    table = np.where(part[:, None] == 0, np.cos(angle), -np.sin(angle))
    table = table.astype(np.float32).astype(jnp.bfloat16).astype(np.float32)
    return (table / math.sqrt(SEGS * BAND)).astype(jnp.bfloat16)


def in_vmem(array):
    return pltpu.with_memory_space_constraint(array, pltpu.VMEM)


def dot(left, right, left_dim=1, right_dim=0):
    return lax.dot_general(
        left, right, (((left_dim,), (right_dim,)), ((), ())), preferred_element_type=F32
    )


def low_lanes(shape):
    return lax.broadcasted_iota(jnp.int32, shape, 1) < BLOCK


def sort_kernel(order_ref, raw_ref, out_ref, raw_low):
    channels = raw_ref.shape[0]
    raw_low[...] = raw_ref[...].astype(BF16)
    lanes = lax.broadcasted_iota(jnp.int32, (128, 128), 1)
    for chunk in range(channels // 128):
        wanted = jnp.broadcast_to(order_ref[chunk : chunk + 1, :], (128, 128)).T
        pieces = [
            jnp.where(wanted == lanes + 128 * piece, 1.0, 0.0).astype(BF16)
            for piece in range(channels // 128)
        ]
        picked = dot(jnp.concatenate(pieces, axis=1), raw_low[...])
        out_ref[pl.ds(chunk * 128, 128), :] = picked.astype(BF16)


def sort_rows(raw, order):
    channels, samples = raw.shape
    return pl.pallas_call(
        sort_kernel,
        out_shape=pltpu.VMEM((channels, samples), BF16),
        in_specs=[pl.BlockSpec(memory_space=pltpu.VMEM)] * 2,
        out_specs=pl.BlockSpec(memory_space=pltpu.VMEM),
        scratch_shapes=[pltpu.VMEM((channels, samples), BF16)],
        name="sort_rows",
    )(order.reshape(channels // 128, 128), raw)


def whiten_kernel(x_ref, band_ref, dft_ref, smooth_ref, scale_ref, out_ref, held):
    low = low_lanes((BAND, 2 * BLOCK))
    half_seg = SEG_LEN // 2
    rows = 2 * BLOCK
    for pair in range(SEGS // 2):
        start = pair * rows
        stop = start + rows
        x = x_ref[start:stop, :]
        size = jnp.abs(x)
        blank = jnp.zeros((BLOCK, half_seg), BF16)
        before = jnp.abs(x_ref[start - BLOCK : start, half_seg:]) if pair > 0 else blank
        after = jnp.abs(x_ref[stop : stop + BLOCK, :half_seg]) if stop < ROWS else blank
        before = jnp.concatenate([before, size[: rows - BLOCK, half_seg:]], axis=0)
        after = jnp.concatenate([size[BLOCK:, :half_seg], after], axis=0)
        around = jnp.concatenate([before, size, after], axis=1)
        mean = dot(around, band_ref[...]) * (1.0 / (2 * NORM_HALF + 1))
        normed = (x.astype(F32) / (mean + 1e-05)).astype(BF16)
        both = dot(normed, dft_ref[...])
        spectrum = both[:, : 2 * BAND] + both[:, 2 * BAND :]
        power = (spectrum * spectrum).astype(BF16)
        smoothed = dot(power, smooth_ref[...])
        white = spectrum * (scale_ref[1:2, :] * lax.rsqrt(smoothed * scale_ref[0:1, :] + 1e-06))
        white = white.T
        lower, upper = white[:BAND], white[BAND:]
        turned = pltpu.roll(jnp.where(low, upper, lower), BLOCK, 1)
        first = jnp.where(low, lower, turned)
        second = jnp.where(low, turned, upper)
        for segment, value in ((2 * pair, first), (2 * pair + 1, second)):
            for part in range(2):
                held[pl.ds(part * SEGS + segment, HALF, stride=2 * SEGS), :] = value[
                    part * HALF : (part + 1) * HALF
                ]
    out_ref[...] = held[...].astype(BF16)


def whiten(x):
    band, dft = band_table(), dft_table()
    smooth, scale = smooth_tables()
    return pl.pallas_call(
        whiten_kernel,
        out_shape=pltpu.VMEM((ROWS, 2 * BLOCK), BF16),
        in_specs=[pl.BlockSpec(memory_space=pltpu.VMEM)] * 5,
        out_specs=pl.BlockSpec(memory_space=pltpu.VMEM),
        scratch_shapes=[pltpu.VMEM((ROWS, 2 * BLOCK), F32)],
        name="whiten",
    )(x, *(in_vmem(jnp.asarray(table)) for table in (band, dft, smooth, scale)))


def fill_cross(left_at, right_at, cross):
    low = low_lanes((2 * SEGS, 2 * BLOCK))
    for place in range(HALF):
        rows = pl.ds(place * 2 * SEGS, 2 * SEGS)
        left = left_at(rows).astype(F32)
        right = right_at(rows).astype(F32)
        other = jnp.concatenate([left[SEGS:], -left[:SEGS]], axis=0)
        turned = pltpu.roll(jnp.where(low, other, left), BLOCK, 1)
        left = jnp.concatenate(
            [jnp.where(low, left, turned), jnp.where(low, turned, other)], axis=0
        ).astype(BF16)
        right = jnp.concatenate(
            [jnp.where(low, right, 0.0), jnp.where(low, 0.0, right)], axis=0
        ).astype(BF16)
        value = dot(left, right, 0, 0)
        for part in range(2):
            cross[pl.ds((2 * place + part) * PITCH, BLOCK), :] = value[part * BLOCK : (part + 1) * BLOCK]


def fill_lags(cross, lag_ref, stage, out, sem):
    low = low_lanes((2 * HALF, 2 * BLOCK))
    copies = []
    for pair in range(BLOCK // 2):
        first = cross[pl.ds(2 * pair, 2 * HALF, stride=PITCH), :]
        second = cross[pl.ds(2 * pair + 1, 2 * HALF, stride=PITCH), :]
        turned = pltpu.roll(jnp.where(low, second, first), BLOCK, 1)
        both = jnp.concatenate(
            [jnp.where(low, first, turned), jnp.where(low, turned, second)], axis=0
        ).T.astype(BF16)
        rows = slice(2 * pair * BLOCK, 2 * (pair + 1) * BLOCK)
        stage[rows, :] = dot(both, lag_ref[...]).astype(BF16)
        if (pair + 1) % STEP == 0:
            done = pl.ds((pair + 1 - STEP) * 2 * BLOCK, STEP * 2 * BLOCK)
            copy = pltpu.make_async_copy(stage.at[done, :], out.at[done, :], sem.at[pair // STEP])
            copy.start()
            copies.append(copy)
    for copy in copies:
        copy.wait()


def diagonal_slot(tiles_ref, own, last):
    position = lax.broadcasted_iota(jnp.int32, (1, tiles_ref.shape[1]), 1)

    def place_of(first, second):
        found = (tiles_ref[0:1, :] == first) & (tiles_ref[1:2, :] == second)
        return jnp.sum(jnp.where(found, position, 0))

    diagonal = place_of(own - 1, own - 1)
    other = place_of(own, jnp.minimum(own + 1, last))
    return jnp.where((own > 0) & (diagonal < other), 0, 1)


def tile_kernel(swap, tiles_ref, own_ref, other_ref, lag_ref, *rest):
    out_ref, cross, stage, sem = rest[-4:]
    own = lax.axis_index("grp") * lax.axis_size("tm") + lax.axis_index("tm")
    last = lax.axis_size("grp") * lax.axis_size("tm") - 1
    is_diagonal = own % 2 == (1 if swap == 0 else 0)
    no_other = (own == last) if swap == 1 else False

    def left_at(rows):
        return jnp.where(is_diagonal, other_ref[rows, :].astype(F32), own_ref[rows, :].astype(F32))

    def right_at(rows):
        if swap == 0:
            return other_ref[rows, :]
        return jnp.where(no_other, own_ref[rows, :].astype(F32), other_ref[rows, :].astype(F32))

    fill_cross(left_at, right_at, cross)
    slot = diagonal_slot(tiles_ref, own, last)
    slot = jnp.where(is_diagonal, slot, 1 - slot)
    fill_lags(cross, lag_ref, stage, out_ref.at[slot], sem)


def correlate(swap, tiles, own, other, held=()):
    vmem = pl.BlockSpec(memory_space=pltpu.VMEM)
    anywhere = pl.BlockSpec(memory_space=pl.ANY)
    return pl.pallas_call(
        lambda *refs: tile_kernel(swap, *refs),
        out_shape=jax.ShapeDtypeStruct((TILE_CAP, BLOCK * BLOCK, LAGS), BF16),
        in_specs=[vmem] * 4 + [anywhere] * len(held),
        out_specs=anywhere,
        scratch_shapes=[
            pltpu.VMEM((HALF * 2 * PITCH, 2 * BLOCK), F32),
            pltpu.VMEM((BLOCK * BLOCK, LAGS), BF16),
            pltpu.SemaphoreType.DMA((BLOCK // 2 // STEP,)),
        ],
        input_output_aliases={4: 0} if held else {},
        name=f"correlate_{swap}",
    )(tiles, own, other, in_vmem(jnp.asarray(lag_table())), *held)


def per_device(raw, channel_order, tile_list, tile_owner):
    count = lax.axis_size("grp") * lax.axis_size("tm")
    ordered = sort_rows(raw, channel_order[0])
    parts = ordered.reshape(SEGS, BLOCK, SEG_LEN)
    record = lax.all_to_all(parts, "tm", split_axis=0, concat_axis=0, tiled=True)
    record = in_vmem(record.reshape(ROWS, SEG_LEN))
    own = in_vmem(whiten(record))
    pairs = [(i, i ^ 1) for i in range(count)]
    shifted = [(i, i + 1 if i % 2 else i - 1) for i in range(1, count - 1)]
    near = in_vmem(lax.ppermute(own, ("grp", "tm"), pairs))
    far = in_vmem(lax.ppermute(own, ("grp", "tm"), shifted))
    tiles = in_vmem(tile_list.T)
    out = correlate(0, tiles, own, near)
    out = correlate(1, tiles, own, far, (out,))
    return out.reshape(TILE_CAP, BLOCK, BLOCK, LAGS)


def solution(mesh):
    return jax.shard_map(
        per_device,
        mesh=mesh,
        in_specs=(P("grp", "tm"), P("grp", None), P(), P()),
        out_specs=P(("grp", "tm"), None, None, None),
        check_vma=False,
    )
```

```python
import math

import jax
import jax.numpy as jnp
import numpy as np
from jax import lax
from jax.experimental import pallas as pl
from jax.experimental.pallas import tpu as pltpu
from jax.sharding import PartitionSpec as P

SEG_LEN = 256
BAND = 64
BAND_LO = 3
LAGS = 128
NORM_HALF = 64
TILE_CAP = 2
BLOCK = 64
SEGS = 16
HALF = BAND // 2
PITCH = 72
STEP = 4
CHUNK = 1024
PITCH2 = 40
ROWS = SEGS * BLOCK
F32 = jnp.float32
BF16 = jnp.bfloat16


def split_bf16(values):
    high = values.astype(jnp.bfloat16)
    low = (values.astype(np.float32) - high.astype(np.float32)).astype(jnp.bfloat16)
    return high, low


def band_table():
    source = np.arange(2 * SEG_LEN) - SEG_LEN // 2
    target = np.arange(SEG_LEN)
    return (np.abs(source[:, None] - target[None, :]) <= NORM_HALF).astype(jnp.bfloat16)


def frequency_rows():
    row = np.arange(2 * BAND)
    upper, part, place = row // BAND, (row // HALF) % 2, row % HALF
    return upper * HALF + place, part


def dft_table():
    freq, part = frequency_rows()
    sample = np.arange(SEG_LEN)
    angle = (sample[:, None] * (freq[None, :] + BAND_LO) % SEG_LEN) * (2.0 * math.pi / SEG_LEN)
    table = np.where(part[None, :] == 0, np.cos(angle), -np.sin(angle)).astype(np.float32)
    return np.concatenate(split_bf16(table), axis=1)


def smooth_tables():
    freq, _ = frequency_rows()
    weights = (BAND - np.abs(freq[:, None] - freq[None, :])).astype(np.float32)
    band = np.arange(BAND)
    total = (BAND - np.abs(band[:, None] - band[None, :])).sum(axis=0).astype(np.float32)
    taper = 0.5 - 0.5 * np.cos((freq + 0.5) * (2.0 * math.pi / BAND))
    scale = np.stack([1.0 / total[freq], taper] * 4).astype(np.float32)
    return weights.astype(jnp.bfloat16), scale


def lag_table():
    row = np.arange(2 * BAND)
    upper, place, part = row // BAND, (row // 2) % HALF, row % 2
    freq = upper * HALF + place + BAND_LO
    lag = np.arange(LAGS) - LAGS // 2
    angle = (freq[:, None] * lag[None, :] % SEG_LEN) * (2.0 * math.pi / SEG_LEN)
    table = np.where(part[:, None] == 0, np.cos(angle), -np.sin(angle))
    table = table.astype(np.float32).astype(jnp.bfloat16).astype(np.float32)
    return (table / math.sqrt(SEGS * BAND)).astype(jnp.bfloat16)


def in_vmem(array):
    return pltpu.with_memory_space_constraint(array, pltpu.VMEM)


def dot(left, right, left_dim=1, right_dim=0):
    return lax.dot_general(
        left, right, (((left_dim,), (right_dim,)), ((), ())), preferred_element_type=F32
    )


def low_lanes(shape):
    return lax.broadcasted_iota(jnp.int32, shape, 1) < BLOCK


def sort_kernel(order_ref, raw_ref, out_ref, raw_low):
    channels = raw_ref.shape[0]
    raw_low[...] = raw_ref[...].astype(BF16)
    lanes = lax.broadcasted_iota(jnp.int32, (128, 128), 1)
    for chunk in range(channels // 128):
        wanted = jnp.broadcast_to(order_ref[chunk : chunk + 1, :], (128, 128)).T
        pieces = [
            jnp.where(wanted == lanes + 128 * piece, 1.0, 0.0).astype(BF16)
            for piece in range(channels // 128)
        ]
        picked = dot(jnp.concatenate(pieces, axis=1), raw_low[...])
        out_ref[pl.ds(chunk * 128, 128), :] = picked.astype(BF16)


def sort_rows(raw, order):
    channels, samples = raw.shape
    return pl.pallas_call(
        sort_kernel,
        out_shape=pltpu.VMEM((channels, samples), BF16),
        in_specs=[pl.BlockSpec(memory_space=pltpu.VMEM)] * 2,
        out_specs=pl.BlockSpec(memory_space=pltpu.VMEM),
        scratch_shapes=[pltpu.VMEM((channels, samples), BF16)],
        name="sort_rows",
    )(order.reshape(channels // 128, 128), raw)


def whiten_kernel(x_ref, band_ref, dft_ref, smooth_ref, scale_ref, out_ref, held):
    low = low_lanes((BAND, 2 * BLOCK))
    half_seg = SEG_LEN // 2
    rows = CHUNK
    blank = jnp.zeros((BLOCK, half_seg), BF16)
    for start in range(0, ROWS, rows):
        stop = start + rows
        x = x_ref[start:stop, :]
        size = jnp.abs(x)
        before = jnp.abs(x_ref[start - BLOCK : start, half_seg:]) if start > 0 else blank
        after = jnp.abs(x_ref[stop : stop + BLOCK, :half_seg]) if stop < ROWS else blank
        before = jnp.concatenate([before, size[: rows - BLOCK, half_seg:]], axis=0)
        after = jnp.concatenate([size[BLOCK:, :half_seg], after], axis=0)
        around = jnp.concatenate([before, size, after], axis=1)
        mean = dot(around, band_ref[...]) * (1.0 / (2 * NORM_HALF + 1))
        normed = (x.astype(F32) / (mean + 1e-05)).astype(BF16)
        both = dot(normed, dft_ref[...])
        spectrum = both[:, : 2 * BAND] + both[:, 2 * BAND :]
        power = (spectrum * spectrum).astype(BF16)
        smoothed = dot(power, smooth_ref[...])
        whites = spectrum * (scale_ref[1:2, :] * lax.rsqrt(smoothed * scale_ref[0:1, :] + 1e-06))
        for inner in range(0, rows, 2 * BLOCK):
            segment = (start + inner) // BLOCK
            white = whites[inner : inner + 2 * BLOCK].T
            lower, upper = white[:BAND], white[BAND:]
            turned = pltpu.roll(jnp.where(low, upper, lower), BLOCK, 1)
            first = jnp.where(low, lower, turned)
            second = jnp.where(low, turned, upper)
            for number, value in ((segment, first), (segment + 1, second)):
                for part in range(2):
                    held[pl.ds(part * SEGS + number, HALF, stride=PITCH2), :] = value[
                        part * HALF : (part + 1) * HALF
                    ]
    for place in range(HALF):
        out_ref[place * 2 * SEGS : (place + 1) * 2 * SEGS, :] = held[
            place * PITCH2 : place * PITCH2 + 2 * SEGS, :
        ].astype(BF16)


def whiten(x):
    band, dft = band_table(), dft_table()
    smooth, scale = smooth_tables()
    return pl.pallas_call(
        whiten_kernel,
        out_shape=pltpu.VMEM((ROWS, 2 * BLOCK), BF16),
        in_specs=[pl.BlockSpec(memory_space=pltpu.VMEM)] * 5,
        out_specs=pl.BlockSpec(memory_space=pltpu.VMEM),
        scratch_shapes=[pltpu.VMEM((HALF * PITCH2, 2 * BLOCK), F32)],
        name="whiten",
    )(x, *(in_vmem(jnp.asarray(table)) for table in (band, dft, smooth, scale)))


def fill_cross(left_at, right_at, cross):
    low = low_lanes((2 * SEGS, 2 * BLOCK))
    for place in range(HALF):
        rows = pl.ds(place * 2 * SEGS, 2 * SEGS)
        left = left_at(rows).astype(F32)
        right = right_at(rows).astype(F32)
        other = jnp.concatenate([left[SEGS:], -left[:SEGS]], axis=0)
        turned = pltpu.roll(jnp.where(low, other, left), BLOCK, 1)
        left = jnp.concatenate(
            [jnp.where(low, left, turned), jnp.where(low, turned, other)], axis=0
        ).astype(BF16)
        right = jnp.concatenate(
            [jnp.where(low, right, 0.0), jnp.where(low, 0.0, right)], axis=0
        ).astype(BF16)
        value = dot(left, right, 0, 0)
        for part in range(2):
            cross[pl.ds((2 * place + part) * PITCH, BLOCK), :] = value[part * BLOCK : (part + 1) * BLOCK]


def fill_lags(cross, lag_ref, stage, out, sem):
    low = low_lanes((2 * HALF, 2 * BLOCK))
    copies = []
    for pair in range(BLOCK // 2):
        first = cross[pl.ds(2 * pair, 2 * HALF, stride=PITCH), :]
        second = cross[pl.ds(2 * pair + 1, 2 * HALF, stride=PITCH), :]
        turned = pltpu.roll(jnp.where(low, second, first), BLOCK, 1)
        both = jnp.concatenate(
            [jnp.where(low, first, turned), jnp.where(low, turned, second)], axis=0
        ).T.astype(BF16)
        rows = slice(2 * pair * BLOCK, 2 * (pair + 1) * BLOCK)
        stage[rows, :] = dot(both, lag_ref[...]).astype(BF16)
        if (pair + 1) % STEP == 0:
            done = pl.ds((pair + 1 - STEP) * 2 * BLOCK, STEP * 2 * BLOCK)
            copy = pltpu.make_async_copy(stage.at[done, :], out.at[done, :], sem.at[pair // STEP])
            copy.start()
            copies.append(copy)
    for copy in copies:
        copy.wait()


def diagonal_slot(tiles_ref, own, last):
    position = lax.broadcasted_iota(jnp.int32, (1, tiles_ref.shape[1]), 1)

    def place_of(first, second):
        found = (tiles_ref[0:1, :] == first) & (tiles_ref[1:2, :] == second)
        return jnp.sum(jnp.where(found, position, 0))

    diagonal = place_of(own - 1, own - 1)
    other = place_of(own, jnp.minimum(own + 1, last))
    return jnp.where((own > 0) & (diagonal < other), 0, 1)


def tile_kernel(swap, tiles_ref, own_ref, other_ref, lag_ref, *rest):
    out_ref, cross, stage, sem = rest[-4:]
    own = lax.axis_index("grp") * lax.axis_size("tm") + lax.axis_index("tm")
    last = lax.axis_size("grp") * lax.axis_size("tm") - 1
    is_diagonal = own % 2 == (1 if swap == 0 else 0)
    no_other = (own == last) if swap == 1 else False

    def left_at(rows):
        return jnp.where(is_diagonal, other_ref[rows, :].astype(F32), own_ref[rows, :].astype(F32))

    def right_at(rows):
        if swap == 0:
            return other_ref[rows, :]
        return jnp.where(no_other, own_ref[rows, :].astype(F32), other_ref[rows, :].astype(F32))

    fill_cross(left_at, right_at, cross)
    slot = diagonal_slot(tiles_ref, own, last)
    slot = jnp.where(is_diagonal, slot, 1 - slot)
    fill_lags(cross, lag_ref, stage, out_ref.at[slot], sem)


def correlate(swap, tiles, own, other, held=()):
    vmem = pl.BlockSpec(memory_space=pltpu.VMEM)
    anywhere = pl.BlockSpec(memory_space=pl.ANY)
    return pl.pallas_call(
        lambda *refs: tile_kernel(swap, *refs),
        out_shape=jax.ShapeDtypeStruct((TILE_CAP, BLOCK * BLOCK, LAGS), BF16),
        in_specs=[vmem] * 4 + [anywhere] * len(held),
        out_specs=anywhere,
        scratch_shapes=[
            pltpu.VMEM((HALF * 2 * PITCH, 2 * BLOCK), F32),
            pltpu.VMEM((BLOCK * BLOCK, LAGS), BF16),
            pltpu.SemaphoreType.DMA((BLOCK // 2 // STEP,)),
        ],
        input_output_aliases={4: 0} if held else {},
        name=f"correlate_{swap}",
    )(tiles, own, other, in_vmem(jnp.asarray(lag_table())), *held)


def per_device(raw, channel_order, tile_list, tile_owner):
    count = lax.axis_size("grp") * lax.axis_size("tm")
    ordered = sort_rows(raw, channel_order[0])
    parts = ordered.reshape(SEGS, BLOCK, SEG_LEN)
    record = lax.all_to_all(parts, "tm", split_axis=0, concat_axis=0, tiled=True)
    record = in_vmem(record.reshape(ROWS, SEG_LEN))
    own = in_vmem(whiten(record))
    pairs = [(i, i ^ 1) for i in range(count)]
    shifted = [(i, i + 1 if i % 2 else i - 1) for i in range(1, count - 1)]
    near = in_vmem(lax.ppermute(own, ("grp", "tm"), pairs))
    far = in_vmem(lax.ppermute(own, ("grp", "tm"), shifted))
    tiles = in_vmem(tile_list.T)
    out = correlate(0, tiles, own, near)
    out = correlate(1, tiles, own, far, (out,))
    return out.reshape(TILE_CAP, BLOCK, BLOCK, LAGS)


def solution(mesh):
    return jax.shard_map(
        per_device,
        mesh=mesh,
        in_specs=(P("grp", "tm"), P("grp", None), P(), P()),
        out_specs=P(("grp", "tm"), None, None, None),
        check_vma=False,
    )
```

```python
import math

import jax
import jax.numpy as jnp
import numpy as np
from jax import lax
from jax.experimental import pallas as pl
from jax.experimental.pallas import tpu as pltpu
from jax.sharding import PartitionSpec as P

SEG_LEN = 256
BAND = 64
BAND_LO = 3
LAGS = 128
NORM_HALF = 64
TILE_CAP = 2
BLOCK = 64
SEGS = 16
HALF = BAND // 2
PITCH = 65
STEP = 4
CHUNK = 1024
PITCH2 = 33
ROWS = SEGS * BLOCK
F32 = jnp.float32
BF16 = jnp.bfloat16


def split_bf16(values):
    high = values.astype(jnp.bfloat16)
    low = (values.astype(np.float32) - high.astype(np.float32)).astype(jnp.bfloat16)
    return high, low


def band_table():
    source = np.arange(2 * SEG_LEN) - SEG_LEN // 2
    target = np.arange(SEG_LEN)
    return (np.abs(source[:, None] - target[None, :]) <= NORM_HALF).astype(jnp.bfloat16)


def frequency_rows():
    row = np.arange(2 * BAND)
    upper, part, place = row // BAND, (row // HALF) % 2, row % HALF
    return upper * HALF + place, part


def dft_table():
    freq, part = frequency_rows()
    sample = np.arange(SEG_LEN)
    angle = (sample[:, None] * (freq[None, :] + BAND_LO) % SEG_LEN) * (2.0 * math.pi / SEG_LEN)
    table = np.where(part[None, :] == 0, np.cos(angle), -np.sin(angle)).astype(np.float32)
    return np.concatenate(split_bf16(table), axis=1)


def smooth_tables():
    freq, _ = frequency_rows()
    weights = (BAND - np.abs(freq[:, None] - freq[None, :])).astype(np.float32)
    band = np.arange(BAND)
    total = (BAND - np.abs(band[:, None] - band[None, :])).sum(axis=0).astype(np.float32)
    taper = 0.5 - 0.5 * np.cos((freq + 0.5) * (2.0 * math.pi / BAND))
    scale = np.stack([1.0 / total[freq], taper] * 4).astype(np.float32)
    return weights.astype(jnp.bfloat16), scale


def lag_table():
    row = np.arange(2 * BAND)
    upper, place, part = row // BAND, (row // 2) % HALF, row % 2
    freq = upper * HALF + place + BAND_LO
    lag = np.arange(LAGS) - LAGS // 2
    angle = (freq[:, None] * lag[None, :] % SEG_LEN) * (2.0 * math.pi / SEG_LEN)
    table = np.where(part[:, None] == 0, np.cos(angle), -np.sin(angle))
    table = table.astype(np.float32).astype(jnp.bfloat16).astype(np.float32)
    return (table / math.sqrt(SEGS * BAND)).astype(jnp.bfloat16)


def in_vmem(array):
    return pltpu.with_memory_space_constraint(array, pltpu.VMEM)


def dot(left, right, left_dim=1, right_dim=0):
    return lax.dot_general(
        left, right, (((left_dim,), (right_dim,)), ((), ())), preferred_element_type=F32
    )


def low_lanes(shape):
    return lax.broadcasted_iota(jnp.int32, shape, 1) < BLOCK


def pick_kernel(order_ref, out_ref):
    lanes = lax.broadcasted_iota(jnp.int32, (128, 128), 1)
    for chunk in range(out_ref.shape[0] // 128):
        wanted = jnp.broadcast_to(order_ref[chunk : chunk + 1, :], (128, 128)).T
        for piece in range(out_ref.shape[1] // 128):
            out_ref[chunk * 128 : (chunk + 1) * 128, piece * 128 : (piece + 1) * 128] = jnp.where(
                wanted == lanes + 128 * piece, 1.0, 0.0
            ).astype(BF16)


def sort_kernel(picks_ref, raw_ref, out_ref):
    out_ref[...] = dot(picks_ref[...], raw_ref[...].astype(BF16)).astype(BF16)


def sort_rows(raw, order):
    channels, samples = raw.shape
    vmem = pl.BlockSpec(memory_space=pltpu.VMEM)
    picks = pl.pallas_call(
        pick_kernel,
        out_shape=pltpu.VMEM((channels, channels), BF16),
        in_specs=[vmem],
        out_specs=vmem,
        compiler_params=pltpu.CompilerParams(vmem_limit_bytes=16 << 20),
        name="pick_rows",
    )(in_vmem(order.reshape(channels // 128, 128)))
    return pl.pallas_call(
        sort_kernel,
        out_shape=pltpu.VMEM((channels, samples), BF16),
        in_specs=[vmem] * 2,
        out_specs=vmem,
        compiler_params=pltpu.CompilerParams(vmem_limit_bytes=16 << 20),
        name="sort_rows",
    )(in_vmem(picks), in_vmem(raw))


def whiten_kernel(x_ref, band_ref, dft_ref, smooth_ref, scale_ref, out_ref, held):
    low = low_lanes((BAND, 2 * BLOCK))
    half_seg = SEG_LEN // 2
    rows = CHUNK
    blank = jnp.zeros((BLOCK, half_seg), BF16)
    for start in range(0, ROWS, rows):
        stop = start + rows
        x = x_ref[start:stop, :]
        size = jnp.abs(x)
        before = jnp.abs(x_ref[start - BLOCK : start, half_seg:]) if start > 0 else blank
        after = jnp.abs(x_ref[stop : stop + BLOCK, :half_seg]) if stop < ROWS else blank
        before = jnp.concatenate([before, size[: rows - BLOCK, half_seg:]], axis=0)
        after = jnp.concatenate([size[BLOCK:, :half_seg], after], axis=0)
        around = jnp.concatenate([before, size, after], axis=1)
        mean = dot(around, band_ref[...]) * (1.0 / (2 * NORM_HALF + 1))
        normed = (x.astype(F32) / (mean + 1e-05)).astype(BF16)
        both = dot(normed, dft_ref[...])
        spectrum = both[:, : 2 * BAND] + both[:, 2 * BAND :]
        power = (spectrum * spectrum).astype(BF16)
        smoothed = dot(power, smooth_ref[...])
        whites = spectrum * (scale_ref[1:2, :] * lax.rsqrt(smoothed * scale_ref[0:1, :] + 1e-06))
        for inner in range(0, rows, 2 * BLOCK):
            segment = (start + inner) // BLOCK
            white = whites[inner : inner + 2 * BLOCK].T
            lower, upper = white[:BAND], white[BAND:]
            turned = pltpu.roll(jnp.where(low, upper, lower), BLOCK, 1)
            first = jnp.where(low, lower, turned)
            second = jnp.where(low, turned, upper)
            for number, value in ((segment, first), (segment + 1, second)):
                for part in range(2):
                    held[pl.ds(part * SEGS + number, HALF, stride=PITCH2), :] = value[
                        part * HALF : (part + 1) * HALF
                    ]
    for place in range(HALF):
        out_ref[place * 2 * SEGS : (place + 1) * 2 * SEGS, :] = held[
            place * PITCH2 : place * PITCH2 + 2 * SEGS, :
        ].astype(BF16)


def whiten(x):
    band, dft = band_table(), dft_table()
    smooth, scale = smooth_tables()
    return pl.pallas_call(
        whiten_kernel,
        out_shape=pltpu.VMEM((ROWS, 2 * BLOCK), BF16),
        in_specs=[pl.BlockSpec(memory_space=pltpu.VMEM)] * 5,
        out_specs=pl.BlockSpec(memory_space=pltpu.VMEM),
        scratch_shapes=[pltpu.VMEM((HALF * PITCH2, 2 * BLOCK), F32)],
        name="whiten",
    )(x, *(in_vmem(jnp.asarray(table)) for table in (band, dft, smooth, scale)))


def fill_cross(left_at, right_at, cross):
    low = low_lanes((2 * SEGS, 2 * BLOCK))
    for place in range(HALF):
        rows = pl.ds(place * 2 * SEGS, 2 * SEGS)
        left = left_at(rows).astype(F32)
        right = right_at(rows).astype(F32)
        other = jnp.concatenate([left[SEGS:], -left[:SEGS]], axis=0)
        turned = pltpu.roll(jnp.where(low, other, left), BLOCK, 1)
        left = jnp.concatenate(
            [jnp.where(low, left, turned), jnp.where(low, turned, other)], axis=0
        ).astype(BF16)
        right = jnp.concatenate(
            [jnp.where(low, right, 0.0), jnp.where(low, 0.0, right)], axis=0
        ).astype(BF16)
        value = dot(left, right, 0, 0)
        for part in range(2):
            cross[pl.ds((2 * place + part) * PITCH, BLOCK), :] = value[part * BLOCK : (part + 1) * BLOCK]


def fill_lags(cross, lag_ref, stage, out, sem):
    low = low_lanes((2 * HALF, 2 * BLOCK))
    copies = []
    for pair in range(BLOCK // 2):
        first = cross[pl.ds(2 * pair, 2 * HALF, stride=PITCH), :]
        second = cross[pl.ds(2 * pair + 1, 2 * HALF, stride=PITCH), :]
        turned = pltpu.roll(jnp.where(low, second, first), BLOCK, 1)
        both = jnp.concatenate(
            [jnp.where(low, first, turned), jnp.where(low, turned, second)], axis=0
        ).T.astype(BF16)
        rows = slice(2 * pair * BLOCK, 2 * (pair + 1) * BLOCK)
        stage[rows, :] = dot(both, lag_ref[...]).astype(BF16)
        if (pair + 1) % STEP == 0:
            done = pl.ds((pair + 1 - STEP) * 2 * BLOCK, STEP * 2 * BLOCK)
            copy = pltpu.make_async_copy(stage.at[done, :], out.at[done, :], sem.at[pair // STEP])
            copy.start()
            copies.append(copy)
    for copy in copies:
        copy.wait()


def diagonal_slot(tiles_ref, own, last):
    position = lax.broadcasted_iota(jnp.int32, (1, tiles_ref.shape[1]), 1)

    def place_of(first, second):
        found = (tiles_ref[0:1, :] == first) & (tiles_ref[1:2, :] == second)
        return jnp.sum(jnp.where(found, position, 0))

    diagonal = place_of(own - 1, own - 1)
    other = place_of(own, jnp.minimum(own + 1, last))
    return jnp.where((own > 0) & (diagonal < other), 0, 1)


def tile_kernel(swap, tiles_ref, own_ref, other_ref, lag_ref, *rest):
    out_ref, cross, stage, sem = rest[-4:]
    own = lax.axis_index("grp") * lax.axis_size("tm") + lax.axis_index("tm")
    last = lax.axis_size("grp") * lax.axis_size("tm") - 1
    is_diagonal = own % 2 == (1 if swap == 0 else 0)
    no_other = (own == last) if swap == 1 else False

    def left_at(rows):
        return jnp.where(is_diagonal, other_ref[rows, :].astype(F32), own_ref[rows, :].astype(F32))

    def right_at(rows):
        if swap == 0:
            return other_ref[rows, :]
        return jnp.where(no_other, own_ref[rows, :].astype(F32), other_ref[rows, :].astype(F32))

    fill_cross(left_at, right_at, cross)
    slot = diagonal_slot(tiles_ref, own, last)
    slot = jnp.where(is_diagonal, slot, 1 - slot)
    fill_lags(cross, lag_ref, stage, out_ref.at[slot], sem)


def correlate(swap, tiles, own, other, held=()):
    vmem = pl.BlockSpec(memory_space=pltpu.VMEM)
    anywhere = pl.BlockSpec(memory_space=pl.ANY)
    return pl.pallas_call(
        lambda *refs: tile_kernel(swap, *refs),
        out_shape=jax.ShapeDtypeStruct((TILE_CAP, BLOCK * BLOCK, LAGS), BF16),
        in_specs=[vmem] * 4 + [anywhere] * len(held),
        out_specs=anywhere,
        scratch_shapes=[
            pltpu.VMEM((HALF * 2 * PITCH, 2 * BLOCK), F32),
            pltpu.VMEM((BLOCK * BLOCK, LAGS), BF16),
            pltpu.SemaphoreType.DMA((BLOCK // 2 // STEP,)),
        ],
        input_output_aliases={4: 0} if held else {},
        name=f"correlate_{swap}",
    )(tiles, own, other, in_vmem(jnp.asarray(lag_table())), *held)


def per_device(raw, channel_order, tile_list, tile_owner):
    count = lax.axis_size("grp") * lax.axis_size("tm")
    ordered = sort_rows(raw, channel_order[0])
    parts = ordered.reshape(SEGS, BLOCK, SEG_LEN)
    record = lax.all_to_all(parts, "tm", split_axis=0, concat_axis=0, tiled=True)
    record = in_vmem(record.reshape(ROWS, SEG_LEN))
    own = in_vmem(whiten(record))
    pairs = [(i, i ^ 1) for i in range(count)]
    shifted = [(i, i + 1 if i % 2 else i - 1) for i in range(1, count - 1)]
    near = in_vmem(lax.ppermute(own, ("grp", "tm"), pairs))
    far = in_vmem(lax.ppermute(own, ("grp", "tm"), shifted))
    tiles = in_vmem(tile_list.T)
    out = correlate(0, tiles, own, near)
    out = correlate(1, tiles, own, far, (out,))
    return out.reshape(TILE_CAP, BLOCK, BLOCK, LAGS)


def solution(mesh):
    return jax.shard_map(
        per_device,
        mesh=mesh,
        in_specs=(P("grp", "tm"), P("grp", None), P(), P()),
        out_specs=P(("grp", "tm"), None, None, None),
        check_vma=False,
    )
```

```python
import math

import jax
import jax.numpy as jnp
import numpy as np
from jax import lax
from jax.experimental import pallas as pl
from jax.experimental.pallas import tpu as pltpu
from jax.sharding import PartitionSpec as P

SEG_LEN = 256
BAND = 64
BAND_LO = 3
LAGS = 128
NORM_HALF = 64
TILE_CAP = 2
BLOCK = 64
SEGS = 16
HALF = BAND // 2
PITCH = 65
STEP = 4
CHUNK = 1024
PITCH2 = 33
ROWS = SEGS * BLOCK
F32 = jnp.float32
BF16 = jnp.bfloat16


def split_bf16(values):
    high = values.astype(jnp.bfloat16)
    low = (values.astype(np.float32) - high.astype(np.float32)).astype(jnp.bfloat16)
    return high, low


def band_table():
    source = np.arange(2 * SEG_LEN) - SEG_LEN // 2
    target = np.arange(SEG_LEN)
    return (np.abs(source[:, None] - target[None, :]) <= NORM_HALF).astype(jnp.bfloat16)


def frequency_rows():
    row = np.arange(2 * BAND)
    upper, part, place = row // BAND, (row // HALF) % 2, row % HALF
    return upper * HALF + place, part


def dft_table():
    freq, part = frequency_rows()
    sample = np.arange(SEG_LEN)
    angle = (sample[:, None] * (freq[None, :] + BAND_LO) % SEG_LEN) * (2.0 * math.pi / SEG_LEN)
    table = np.where(part[None, :] == 0, np.cos(angle), -np.sin(angle)).astype(np.float32)
    return np.concatenate(split_bf16(table), axis=1)


def smooth_tables():
    freq, _ = frequency_rows()
    weights = (BAND - np.abs(freq[:, None] - freq[None, :])).astype(np.float32)
    band = np.arange(BAND)
    total = (BAND - np.abs(band[:, None] - band[None, :])).sum(axis=0).astype(np.float32)
    taper = 0.5 - 0.5 * np.cos((freq + 0.5) * (2.0 * math.pi / BAND))
    scale = np.stack([1.0 / total[freq], taper] * 4).astype(np.float32)
    return weights.astype(jnp.bfloat16), scale


def lag_table():
    row = np.arange(2 * BAND)
    upper, place, part = row // BAND, (row // 2) % HALF, row % 2
    freq = upper * HALF + place + BAND_LO
    lag = np.arange(LAGS) - LAGS // 2
    angle = (freq[:, None] * lag[None, :] % SEG_LEN) * (2.0 * math.pi / SEG_LEN)
    table = np.where(part[:, None] == 0, np.cos(angle), -np.sin(angle))
    table = table.astype(np.float32).astype(jnp.bfloat16).astype(np.float32)
    table = table / math.sqrt(SEGS * BAND)
    both = np.zeros((2, 2, BAND, 2, LAGS), np.float32)
    for channel in range(2):
        both[:, channel, :, channel, :] = table.reshape(2, BAND, LAGS)
    return both.reshape(4 * BAND, 2 * LAGS).astype(jnp.bfloat16)


def in_vmem(array):
    return pltpu.with_memory_space_constraint(array, pltpu.VMEM)


def dot(left, right, left_dim=1, right_dim=0):
    return lax.dot_general(
        left, right, (((left_dim,), (right_dim,)), ((), ())), preferred_element_type=F32
    )


def low_lanes(shape):
    return lax.broadcasted_iota(jnp.int32, shape, 1) < BLOCK


def pick_kernel(order_ref, out_ref):
    lanes = lax.broadcasted_iota(jnp.int32, (128, 128), 1)
    for chunk in range(out_ref.shape[0] // 128):
        wanted = jnp.broadcast_to(order_ref[chunk : chunk + 1, :], (128, 128)).T
        for piece in range(out_ref.shape[1] // 128):
            out_ref[chunk * 128 : (chunk + 1) * 128, piece * 128 : (piece + 1) * 128] = jnp.where(
                wanted == lanes + 128 * piece, 1.0, 0.0
            ).astype(BF16)


def sort_kernel(picks_ref, raw_ref, out_ref):
    out_ref[...] = dot(picks_ref[...], raw_ref[...].astype(BF16)).astype(BF16)


def sort_rows(raw, order):
    channels, samples = raw.shape
    vmem = pl.BlockSpec(memory_space=pltpu.VMEM)
    picks = pl.pallas_call(
        pick_kernel,
        out_shape=pltpu.VMEM((channels, channels), BF16),
        in_specs=[vmem],
        out_specs=vmem,
        compiler_params=pltpu.CompilerParams(vmem_limit_bytes=16 << 20),
        name="pick_rows",
    )(in_vmem(order.reshape(channels // 128, 128)))
    return pl.pallas_call(
        sort_kernel,
        out_shape=pltpu.VMEM((channels, samples), BF16),
        in_specs=[vmem] * 2,
        out_specs=vmem,
        compiler_params=pltpu.CompilerParams(vmem_limit_bytes=16 << 20),
        name="sort_rows",
    )(in_vmem(picks), in_vmem(raw))


def whiten_kernel(x_ref, band_ref, dft_ref, smooth_ref, scale_ref, out_ref, held):
    low = low_lanes((BAND, 2 * BLOCK))
    half_seg = SEG_LEN // 2
    rows = CHUNK
    blank = jnp.zeros((BLOCK, half_seg), BF16)
    for start in range(0, ROWS, rows):
        stop = start + rows
        x = x_ref[start:stop, :]
        size = jnp.abs(x)
        before = jnp.abs(x_ref[start - BLOCK : start, half_seg:]) if start > 0 else blank
        after = jnp.abs(x_ref[stop : stop + BLOCK, :half_seg]) if stop < ROWS else blank
        before = jnp.concatenate([before, size[: rows - BLOCK, half_seg:]], axis=0)
        after = jnp.concatenate([size[BLOCK:, :half_seg], after], axis=0)
        around = jnp.concatenate([before, size, after], axis=1)
        mean = dot(around, band_ref[...]) * (1.0 / (2 * NORM_HALF + 1))
        normed = (x.astype(F32) / (mean + 1e-05)).astype(BF16)
        both = dot(normed, dft_ref[...])
        spectrum = both[:, : 2 * BAND] + both[:, 2 * BAND :]
        power = (spectrum * spectrum).astype(BF16)
        smoothed = dot(power, smooth_ref[...])
        whites = spectrum * (scale_ref[1:2, :] * lax.rsqrt(smoothed * scale_ref[0:1, :] + 1e-06))
        for inner in range(0, rows, 2 * BLOCK):
            segment = (start + inner) // BLOCK
            white = whites[inner : inner + 2 * BLOCK].T
            lower, upper = white[:BAND], white[BAND:]
            turned = pltpu.roll(jnp.where(low, upper, lower), BLOCK, 1)
            first = jnp.where(low, lower, turned)
            second = jnp.where(low, turned, upper)
            for number, value in ((segment, first), (segment + 1, second)):
                for part in range(2):
                    held[pl.ds(part * SEGS + number, HALF, stride=PITCH2), :] = value[
                        part * HALF : (part + 1) * HALF
                    ]
    for place in range(HALF):
        out_ref[place * 2 * SEGS : (place + 1) * 2 * SEGS, :] = held[
            place * PITCH2 : place * PITCH2 + 2 * SEGS, :
        ].astype(BF16)


def whiten(x):
    band, dft = band_table(), dft_table()
    smooth, scale = smooth_tables()
    return pl.pallas_call(
        whiten_kernel,
        out_shape=pltpu.VMEM((ROWS, 2 * BLOCK), BF16),
        in_specs=[pl.BlockSpec(memory_space=pltpu.VMEM)] * 5,
        out_specs=pl.BlockSpec(memory_space=pltpu.VMEM),
        scratch_shapes=[pltpu.VMEM((HALF * PITCH2, 2 * BLOCK), F32)],
        name="whiten",
    )(x, *(in_vmem(jnp.asarray(table)) for table in (band, dft, smooth, scale)))


def fill_cross(left_at, right_at, cross):
    low = low_lanes((2 * SEGS, 2 * BLOCK))
    for place in range(HALF):
        rows = pl.ds(place * 2 * SEGS, 2 * SEGS)
        left = left_at(rows).astype(F32)
        right = right_at(rows).astype(F32)
        other = jnp.concatenate([left[SEGS:], -left[:SEGS]], axis=0)
        turned = pltpu.roll(jnp.where(low, other, left), BLOCK, 1)
        left = jnp.concatenate(
            [jnp.where(low, left, turned), jnp.where(low, turned, other)], axis=0
        ).astype(BF16)
        right = jnp.concatenate(
            [jnp.where(low, right, 0.0), jnp.where(low, 0.0, right)], axis=0
        ).astype(BF16)
        value = dot(left, right, 0, 0)
        for part in range(2):
            cross[pl.ds((2 * place + part) * PITCH, BLOCK), :] = value[part * BLOCK : (part + 1) * BLOCK]


def fill_lags(cross, lag_ref, stage, out, sem):
    copies = []
    for pair in range(1, BLOCK // 2, 2):
        lefts = []
        for each in range(pair - 1, pair + 1):
            first = cross[pl.ds(2 * each, 2 * HALF, stride=PITCH), :]
            second = cross[pl.ds(2 * each + 1, 2 * HALF, stride=PITCH), :]
            turned = jnp.concatenate([first, second], axis=0).astype(BF16).T
            lefts.append(jnp.concatenate([turned[:BLOCK], turned[BLOCK:]], axis=1))
        values = dot(jnp.concatenate(lefts, axis=0), lag_ref[...]).astype(BF16)
        for number in range(2):
            rows = values[number * BLOCK : (number + 1) * BLOCK]
            start = 2 * (pair - 1 + number) * BLOCK
            stage[start : start + BLOCK, :] = rows[:, :LAGS]
            stage[start + BLOCK : start + 2 * BLOCK, :] = rows[:, LAGS:]
        if (pair + 1) % STEP == 0:
            done = pl.ds((pair + 1 - STEP) * 2 * BLOCK, STEP * 2 * BLOCK)
            copy = pltpu.make_async_copy(stage.at[done, :], out.at[done, :], sem.at[pair // STEP])
            copy.start()
            copies.append(copy)
    for copy in copies:
        copy.wait()


def diagonal_slot(tiles_ref, own, last):
    position = lax.broadcasted_iota(jnp.int32, (1, tiles_ref.shape[1]), 1)

    def place_of(first, second):
        found = (tiles_ref[0:1, :] == first) & (tiles_ref[1:2, :] == second)
        return jnp.sum(jnp.where(found, position, 0))

    diagonal = place_of(own - 1, own - 1)
    other = place_of(own, jnp.minimum(own + 1, last))
    return jnp.where((own > 0) & (diagonal < other), 0, 1)


def tile_kernel(swap, tiles_ref, own_ref, other_ref, lag_ref, *rest):
    out_ref, cross, stage, sem = rest[-4:]
    own = lax.axis_index("grp") * lax.axis_size("tm") + lax.axis_index("tm")
    last = lax.axis_size("grp") * lax.axis_size("tm") - 1
    is_diagonal = own % 2 == (1 if swap == 0 else 0)
    no_other = (own == last) if swap == 1 else False

    def left_at(rows):
        return jnp.where(is_diagonal, other_ref[rows, :].astype(F32), own_ref[rows, :].astype(F32))

    def right_at(rows):
        if swap == 0:
            return other_ref[rows, :]
        return jnp.where(no_other, own_ref[rows, :].astype(F32), other_ref[rows, :].astype(F32))

    fill_cross(left_at, right_at, cross)
    slot = diagonal_slot(tiles_ref, own, last)
    slot = jnp.where(is_diagonal, slot, 1 - slot)
    fill_lags(cross, lag_ref, stage, out_ref.at[slot], sem)


def correlate(swap, tiles, own, other, held=()):
    vmem = pl.BlockSpec(memory_space=pltpu.VMEM)
    anywhere = pl.BlockSpec(memory_space=pl.ANY)
    return pl.pallas_call(
        lambda *refs: tile_kernel(swap, *refs),
        out_shape=jax.ShapeDtypeStruct((TILE_CAP, BLOCK * BLOCK, LAGS), BF16),
        in_specs=[vmem] * 4 + [anywhere] * len(held),
        out_specs=anywhere,
        scratch_shapes=[
            pltpu.VMEM((HALF * 2 * PITCH, 2 * BLOCK), F32),
            pltpu.VMEM((BLOCK * BLOCK, LAGS), BF16),
            pltpu.SemaphoreType.DMA((BLOCK // 2 // STEP,)),
        ],
        input_output_aliases={4: 0} if held else {},
        name=f"correlate_{swap}",
    )(tiles, own, other, in_vmem(jnp.asarray(lag_table())), *held)


def per_device(raw, channel_order, tile_list, tile_owner):
    count = lax.axis_size("grp") * lax.axis_size("tm")
    ordered = sort_rows(raw, channel_order[0])
    parts = ordered.reshape(SEGS, BLOCK, SEG_LEN)
    record = lax.all_to_all(parts, "tm", split_axis=0, concat_axis=0, tiled=True)
    record = in_vmem(record.reshape(ROWS, SEG_LEN))
    own = in_vmem(whiten(record))
    pairs = [(i, i ^ 1) for i in range(count)]
    shifted = [(i, i + 1 if i % 2 else i - 1) for i in range(1, count - 1)]
    near = in_vmem(lax.ppermute(own, ("grp", "tm"), pairs))
    far = in_vmem(lax.ppermute(own, ("grp", "tm"), shifted))
    tiles = in_vmem(tile_list.T)
    out = correlate(0, tiles, own, near)
    out = correlate(1, tiles, own, far, (out,))
    return out.reshape(TILE_CAP, BLOCK, BLOCK, LAGS)


def solution(mesh):
    return jax.shard_map(
        per_device,
        mesh=mesh,
        in_specs=(P("grp", "tm"), P("grp", None), P(), P()),
        out_specs=P(("grp", "tm"), None, None, None),
        check_vma=False,
    )
```

```python
import math

import jax
import jax.numpy as jnp
import numpy as np
from jax import lax
from jax.experimental import pallas as pl
from jax.experimental.pallas import tpu as pltpu
from jax.sharding import PartitionSpec as P

SEG_LEN = 256
BAND = 64
BAND_LO = 3
LAGS = 128
NORM_HALF = 64
TILE_CAP = 2
BLOCK = 64
SEGS = 16
HALF = BAND // 2
PITCH = 65
STEP = 8
CHUNK = 1024
PITCH2 = 33
ROWS = SEGS * BLOCK
F32 = jnp.float32
BF16 = jnp.bfloat16


def split_bf16(values):
    high = values.astype(jnp.bfloat16)
    low = (values.astype(np.float32) - high.astype(np.float32)).astype(jnp.bfloat16)
    return high, low


def band_table():
    source = np.arange(2 * SEG_LEN) - SEG_LEN // 2
    target = np.arange(SEG_LEN)
    return (np.abs(source[:, None] - target[None, :]) <= NORM_HALF).astype(jnp.bfloat16)


def frequency_rows():
    row = np.arange(2 * BAND)
    upper, part, place = row // BAND, (row // HALF) % 2, row % HALF
    return upper * HALF + place, part


def dft_table():
    freq, part = frequency_rows()
    sample = np.arange(SEG_LEN)
    angle = (sample[:, None] * (freq[None, :] + BAND_LO) % SEG_LEN) * (2.0 * math.pi / SEG_LEN)
    table = np.where(part[None, :] == 0, np.cos(angle), -np.sin(angle)).astype(np.float32)
    return np.concatenate(split_bf16(table), axis=1)


def smooth_tables():
    freq, _ = frequency_rows()
    weights = (BAND - np.abs(freq[:, None] - freq[None, :])).astype(np.float32)
    band = np.arange(BAND)
    total = (BAND - np.abs(band[:, None] - band[None, :])).sum(axis=0).astype(np.float32)
    taper = 0.5 - 0.5 * np.cos((freq + 0.5) * (2.0 * math.pi / BAND))
    scale = np.stack([1.0 / total[freq], taper] * 4).astype(np.float32)
    return weights.astype(jnp.bfloat16), scale


def lag_table():
    row = np.arange(2 * BAND)
    upper, place, part = row // BAND, (row // 2) % HALF, row % 2
    freq = upper * HALF + place + BAND_LO
    lag = np.arange(LAGS) - LAGS // 2
    angle = (freq[:, None] * lag[None, :] % SEG_LEN) * (2.0 * math.pi / SEG_LEN)
    table = np.where(part[:, None] == 0, np.cos(angle), -np.sin(angle))
    table = table.astype(np.float32).astype(jnp.bfloat16).astype(np.float32)
    table = table / math.sqrt(SEGS * BAND)
    both = np.zeros((2, 2, BAND, 2, LAGS), np.float32)
    for channel in range(2):
        both[:, channel, :, channel, :] = table.reshape(2, BAND, LAGS)
    return both.reshape(4 * BAND, 2 * LAGS).astype(jnp.bfloat16)


def in_vmem(array):
    return pltpu.with_memory_space_constraint(array, pltpu.VMEM)


def dot(left, right, left_dim=1, right_dim=0):
    return lax.dot_general(
        left, right, (((left_dim,), (right_dim,)), ((), ())), preferred_element_type=F32
    )


def low_lanes(shape):
    return lax.broadcasted_iota(jnp.int32, shape, 1) < BLOCK


def pick_kernel(order_ref, out_ref):
    lanes = lax.broadcasted_iota(jnp.int32, (128, 128), 1)
    for chunk in range(out_ref.shape[0] // 128):
        wanted = jnp.broadcast_to(order_ref[chunk : chunk + 1, :], (128, 128)).T
        for piece in range(out_ref.shape[1] // 128):
            out_ref[chunk * 128 : (chunk + 1) * 128, piece * 128 : (piece + 1) * 128] = jnp.where(
                wanted == lanes + 128 * piece, 1.0, 0.0
            ).astype(BF16)


def sort_kernel(picks_ref, raw_ref, out_ref):
    out_ref[...] = dot(picks_ref[...], raw_ref[...].astype(BF16)).astype(BF16)


def sort_rows(raw, order):
    channels, samples = raw.shape
    vmem = pl.BlockSpec(memory_space=pltpu.VMEM)
    picks = pl.pallas_call(
        pick_kernel,
        out_shape=pltpu.VMEM((channels, channels), BF16),
        in_specs=[vmem],
        out_specs=vmem,
        compiler_params=pltpu.CompilerParams(vmem_limit_bytes=16 << 20),
        name="pick_rows",
    )(in_vmem(order.reshape(channels // 128, 128)))
    return pl.pallas_call(
        sort_kernel,
        out_shape=pltpu.VMEM((channels, samples), BF16),
        in_specs=[vmem] * 2,
        out_specs=vmem,
        compiler_params=pltpu.CompilerParams(vmem_limit_bytes=16 << 20),
        name="sort_rows",
    )(in_vmem(picks), in_vmem(raw))


def whiten_kernel(x_ref, band_ref, dft_ref, smooth_ref, scale_ref, out_ref, held):
    low = low_lanes((BAND, 2 * BLOCK))
    half_seg = SEG_LEN // 2
    rows = CHUNK
    blank = jnp.zeros((BLOCK, half_seg), BF16)
    for start in range(0, ROWS, rows):
        stop = start + rows
        x = x_ref[start:stop, :]
        size = jnp.abs(x)
        before = jnp.abs(x_ref[start - BLOCK : start, half_seg:]) if start > 0 else blank
        after = jnp.abs(x_ref[stop : stop + BLOCK, :half_seg]) if stop < ROWS else blank
        before = jnp.concatenate([before, size[: rows - BLOCK, half_seg:]], axis=0)
        after = jnp.concatenate([size[BLOCK:, :half_seg], after], axis=0)
        around = jnp.concatenate([before, size, after], axis=1)
        mean = dot(around, band_ref[...]) * (1.0 / (2 * NORM_HALF + 1))
        normed = (x.astype(F32) / (mean + 1e-05)).astype(BF16)
        both = dot(normed, dft_ref[...])
        spectrum = both[:, : 2 * BAND] + both[:, 2 * BAND :]
        power = (spectrum * spectrum).astype(BF16)
        smoothed = dot(power, smooth_ref[...])
        whites = spectrum * (scale_ref[1:2, :] * lax.rsqrt(smoothed * scale_ref[0:1, :] + 1e-06))
        for inner in range(0, rows, 2 * BLOCK):
            segment = (start + inner) // BLOCK
            white = whites[inner : inner + 2 * BLOCK].T
            lower, upper = white[:BAND], white[BAND:]
            turned = pltpu.roll(jnp.where(low, upper, lower), BLOCK, 1)
            first = jnp.where(low, lower, turned)
            second = jnp.where(low, turned, upper)
            for number, value in ((segment, first), (segment + 1, second)):
                for part in range(2):
                    held[pl.ds(part * SEGS + number, HALF, stride=PITCH2), :] = value[
                        part * HALF : (part + 1) * HALF
                    ]
    for place in range(HALF):
        out_ref[place * 2 * SEGS : (place + 1) * 2 * SEGS, :] = held[
            place * PITCH2 : place * PITCH2 + 2 * SEGS, :
        ].astype(BF16)


def whiten(x):
    band, dft = band_table(), dft_table()
    smooth, scale = smooth_tables()
    return pl.pallas_call(
        whiten_kernel,
        out_shape=pltpu.VMEM((ROWS, 2 * BLOCK), BF16),
        in_specs=[pl.BlockSpec(memory_space=pltpu.VMEM)] * 5,
        out_specs=pl.BlockSpec(memory_space=pltpu.VMEM),
        scratch_shapes=[pltpu.VMEM(((HALF + 2) * PITCH2 // 8 * 8, 2 * BLOCK), F32)],
        name="whiten",
    )(x, *(in_vmem(jnp.asarray(table)) for table in (band, dft, smooth, scale)))


def fill_cross(left_at, right_at, cross):
    low = low_lanes((2 * SEGS, 2 * BLOCK))
    for place in range(HALF):
        rows = pl.ds(place * 2 * SEGS, 2 * SEGS)
        left = left_at(rows).astype(F32)
        right = right_at(rows).astype(F32)
        other = jnp.concatenate([left[SEGS:], -left[:SEGS]], axis=0)
        turned = pltpu.roll(jnp.where(low, other, left), BLOCK, 1)
        left = jnp.concatenate(
            [jnp.where(low, left, turned), jnp.where(low, turned, other)], axis=0
        ).astype(BF16)
        right = jnp.concatenate(
            [jnp.where(low, right, 0.0), jnp.where(low, 0.0, right)], axis=0
        ).astype(BF16)
        value = dot(left, right, 0, 0)
        for part in range(2):
            cross[pl.ds((2 * place + part) * PITCH, BLOCK), :] = value[part * BLOCK : (part + 1) * BLOCK]


def fill_lags(cross, lag_ref, stage, out, sem):
    copies = []
    for pair in range(1, BLOCK // 2, 2):
        lefts = []
        for each in range(pair - 1, pair + 1):
            first = cross[pl.ds(2 * each, 2 * HALF, stride=PITCH), :]
            second = cross[pl.ds(2 * each + 1, 2 * HALF, stride=PITCH), :]
            turned = jnp.concatenate([first, second], axis=0).astype(BF16).T
            lefts.append(jnp.concatenate([turned[:BLOCK], turned[BLOCK:]], axis=1))
        values = dot(jnp.concatenate(lefts, axis=0), lag_ref[...]).astype(BF16)
        for number in range(2):
            rows = values[number * BLOCK : (number + 1) * BLOCK]
            start = 2 * (pair - 1 + number) * BLOCK
            stage[start : start + BLOCK, :] = rows[:, :LAGS]
            stage[start + BLOCK : start + 2 * BLOCK, :] = rows[:, LAGS:]
        if (pair + 1) % STEP == 0:
            done = pl.ds((pair + 1 - STEP) * 2 * BLOCK, STEP * 2 * BLOCK)
            copy = pltpu.make_async_copy(stage.at[done, :], out.at[done, :], sem.at[pair // STEP])
            copy.start()
            copies.append(copy)
    for copy in copies:
        copy.wait()


def diagonal_slot(tiles_ref, own, last):
    position = lax.broadcasted_iota(jnp.int32, (1, tiles_ref.shape[1]), 1)

    def place_of(first, second):
        found = (tiles_ref[0:1, :] == first) & (tiles_ref[1:2, :] == second)
        return jnp.sum(jnp.where(found, position, 0))

    diagonal = place_of(own - 1, own - 1)
    other = place_of(own, jnp.minimum(own + 1, last))
    return jnp.where((own > 0) & (diagonal < other), 0, 1)


def tile_kernel(swap, tiles_ref, own_ref, other_ref, lag_ref, *rest):
    out_ref, cross, stage, sem = rest[-4:]
    own = lax.axis_index("grp") * lax.axis_size("tm") + lax.axis_index("tm")
    last = lax.axis_size("grp") * lax.axis_size("tm") - 1
    is_diagonal = own % 2 == (1 if swap == 0 else 0)
    no_other = (own == last) if swap == 1 else False

    def left_at(rows):
        return jnp.where(is_diagonal, other_ref[rows, :].astype(F32), own_ref[rows, :].astype(F32))

    def right_at(rows):
        if swap == 0:
            return other_ref[rows, :]
        return jnp.where(no_other, own_ref[rows, :].astype(F32), other_ref[rows, :].astype(F32))

    fill_cross(left_at, right_at, cross)
    slot = diagonal_slot(tiles_ref, own, last)
    slot = jnp.where(is_diagonal, slot, 1 - slot)
    fill_lags(cross, lag_ref, stage, out_ref.at[slot], sem)


def correlate(swap, tiles, own, other, held=()):
    vmem = pl.BlockSpec(memory_space=pltpu.VMEM)
    anywhere = pl.BlockSpec(memory_space=pl.ANY)
    return pl.pallas_call(
        lambda *refs: tile_kernel(swap, *refs),
        out_shape=jax.ShapeDtypeStruct((TILE_CAP, BLOCK * BLOCK, LAGS), BF16),
        in_specs=[vmem] * 4 + [anywhere] * len(held),
        out_specs=anywhere,
        scratch_shapes=[
            pltpu.VMEM(((2 * HALF + 2) * PITCH // 8 * 8, 2 * BLOCK), F32),
            pltpu.VMEM((BLOCK * BLOCK, LAGS), BF16),
            pltpu.SemaphoreType.DMA((BLOCK // 2 // STEP,)),
        ],
        input_output_aliases={4: 0} if held else {},
        name=f"correlate_{swap}",
    )(tiles, own, other, in_vmem(jnp.asarray(lag_table())), *held)


def per_device(raw, channel_order, tile_list, tile_owner):
    count = lax.axis_size("grp") * lax.axis_size("tm")
    ordered = sort_rows(raw, channel_order[0])
    parts = ordered.reshape(SEGS, BLOCK, SEG_LEN)
    record = lax.all_to_all(parts, "tm", split_axis=0, concat_axis=0, tiled=True)
    record = in_vmem(record.reshape(ROWS, SEG_LEN))
    own = in_vmem(whiten(record))
    pairs = [(i, i ^ 1) for i in range(count)]
    shifted = [(i, i + 1 if i % 2 else i - 1) for i in range(1, count - 1)]
    near = in_vmem(lax.ppermute(own, ("grp", "tm"), pairs))
    far = in_vmem(lax.ppermute(own, ("grp", "tm"), shifted))
    tiles = in_vmem(tile_list.T)
    out = correlate(0, tiles, own, near)
    out = correlate(1, tiles, own, far, (out,))
    return out.reshape(TILE_CAP, BLOCK, BLOCK, LAGS)


def solution(mesh):
    return jax.shard_map(
        per_device,
        mesh=mesh,
        in_specs=(P("grp", "tm"), P("grp", None), P(), P()),
        out_specs=P(("grp", "tm"), None, None, None),
        check_vma=False,
    )
```
